32 devices in a mesh: wide: 8 (over z, y), narrow: 4 (over x, core).
Axes of the slice: x: 2, y: 2, z: 4, core: 2. Of those that a mesh axis runs over, the one named last changes fastest.
Arguments:
- x_prefix: bfloat16 [2048, 2048], P(('wide', 'narrow')), may hold values from -6 to 6
- x_action: bfloat16 [2048, 1024], P(('wide', 'narrow')), may hold values from -6 to 6
- cot_prefix: bfloat16 [2048, 2048], P(('wide', 'narrow')), may hold values from -6 to 6
- cot_action: bfloat16 [2048, 1024], P(('wide', 'narrow')), may hold values from -6 to 6
- prefix_block: int32 [8, 256], P('wide'), may hold values from 0 to 3, never falling along the last dimension, each value on 1 to 128 neighbouring positions
- action_block: int32 [8, 256], P('wide'), may hold values from 0 to 1, never falling along the last dimension, each value on 1 to 255 neighbouring positions
- valid_len: int32 [8], P('wide'), may hold values from 128 to 256
- mix_weight: float32 [8], P('wide'), may hold values from 0.25 to 4
- wq_prefix: bfloat16 [2048, 2048], P('wide', 'narrow'), may hold values from -0.125 to 0.125
- wk_prefix: bfloat16 [2048, 256], P(('wide', 'narrow')), may hold values from -0.125 to 0.125
- wv_prefix: bfloat16 [2048, 256], P(('wide', 'narrow')), may hold values from -0.125 to 0.125
- wo_prefix: bfloat16 [2048, 2048], P('narrow', 'wide'), may hold values from -2 to 2
- wg_prefix: bfloat16 [2048, 16384], P('wide', 'narrow'), may hold values from -0.125 to 0.125
- wu_prefix: bfloat16 [2048, 16384], P('wide', 'narrow'), may hold values from -0.125 to 0.125
- wd_prefix: bfloat16 [16384, 2048], P('narrow', 'wide'), may hold values from -0.046875 to 0.046875
- norm1_prefix: bfloat16 [2048], P(('wide', 'narrow')), may hold values from 0.099609375 to 1.8984375
- norm2_prefix: bfloat16 [2048], P(('wide', 'narrow')), may hold values from 0.099609375 to 1.8984375
- wq_action: bfloat16 [1024, 2048], P('wide', 'narrow'), may hold values from -0.1875 to 0.1875
- wk_action: bfloat16 [1024, 256], P(('wide', 'narrow')), may hold values from -0.1875 to 0.1875
- wv_action: bfloat16 [1024, 256], P(('wide', 'narrow')), may hold values from -0.1875 to 0.1875
- wo_action: bfloat16 [2048, 1024], P('narrow', 'wide'), may hold values from -2 to 2
- wg_action: bfloat16 [1024, 4096], P('wide', 'narrow'), may hold values from -0.1875 to 0.1875
- wu_action: bfloat16 [1024, 4096], P('wide', 'narrow'), may hold values from -0.1875 to 0.1875
- wd_action: bfloat16 [4096, 1024], P('narrow', 'wide'), may hold values from -0.09375 to 0.09375
- norm1_action: bfloat16 [1024], P(('wide', 'narrow')), may hold values from 0.099609375 to 1.8984375
- norm2_action: bfloat16 [1024], P(('wide', 'narrow')), may hold values from 0.099609375 to 1.8984375
Outputs:
- out_prefix: bfloat16 [2048, 2048], P(('wide', 'narrow'))
- out_action: bfloat16 [2048, 1024], P(('wide', 'narrow'))
- grad_x_prefix: float32 [2048, 2048], P(('wide', 'narrow'))
- grad_x_action: float32 [2048, 1024], P(('wide', 'narrow'))
- grad_wq_prefix: float32 [2048, 2048], P('wide', 'narrow')
- grad_wk_prefix: float32 [2048, 256], P(('wide', 'narrow'))
- grad_wv_prefix: float32 [2048, 256], P(('wide', 'narrow'))
- grad_wo_prefix: float32 [2048, 2048], P('narrow', 'wide')
- grad_wg_prefix: float32 [2048, 16384], P('wide', 'narrow')
- grad_wu_prefix: float32 [2048, 16384], P('wide', 'narrow')
- grad_wd_prefix: float32 [16384, 2048], P('narrow', 'wide')
- grad_norm1_prefix: float32 [2048], P(('wide', 'narrow'))
- grad_norm2_prefix: float32 [2048], P(('wide', 'narrow'))
- grad_wq_action: float32 [1024, 2048], P('wide', 'narrow')
- grad_wk_action: float32 [1024, 256], P(('wide', 'narrow'))
- grad_wv_action: float32 [1024, 256], P(('wide', 'narrow'))
- grad_wo_action: float32 [2048, 1024], P('narrow', 'wide')
- grad_wg_action: float32 [1024, 4096], P('wide', 'narrow')
- grad_wu_action: float32 [1024, 4096], P('wide', 'narrow')
- grad_wd_action: float32 [4096, 1024], P('narrow', 'wide')
- grad_norm1_action: float32 [1024], P(('wide', 'narrow'))
- grad_norm2_action: float32 [1024], P(('wide', 'narrow'))
The draws below stay inside these ranges and needn't reach their ends.
Inputs may be any that keep to these rules, and one draw needn't show every extreme that they name: `prefix_block`: within an item the prefix block ids never fall along the tokens, and each of the 4 ids labels at least one token. `action_block`: within an item the action block ids never fall along the tokens, and both ids label at least one token. Prefix keys of an item at positions from valid_len on are padding.
All inputs are finite; a program needn't handle non-finite values.
Results may differ from the reference program's by a relative error of at most 0.018.
Values may be sent and summed in bfloat16 or wider, within the bound.
No kernel may reach another device: no remote copies, remote signals or barrier semaphores. Data moves between devices by JAX's collectives and lax.ppermute only.
A program may use at most 320 MiB of HBM per device.

```python
import math
import jax
import jax.numpy as jnp
import numpy as np
from jax import lax

DP = 2048
FFP = 16384
DA = 1024
FFA = 4096
HEADS = 8
HD = 256
PREFIX_BLOCKS = 4
PRE = 256
ACT = 256
TOK_PREFIX = 2048
TOK_ACTION = 2048
N_WIDE = 8


def touch_ends(values, own_key, smallest, high):
    spot = [jax.random.randint(jax.random.fold_in(own_key, axis), (), 0, length) for axis, length in enumerate(values.shape)]
    longest = values.shape.index(max(values.shape))
    next_to = spot[:longest] + [(spot[longest] + 1) % values.shape[longest]] + spot[longest + 1:]
    return values.at[tuple(spot)].set(smallest).at[tuple(next_to)].set(high)


def block_scale(own_key, dims, cuts, least, largest):
    level = 1.0
    for dim, shards_of in cuts:
        heights = jax.random.uniform(jax.random.fold_in(jax.random.fold_in(own_key, 6), dim), (shards_of,), jnp.float32, least / len(cuts), largest / len(cuts))
        level = level * jnp.repeat(jnp.exp(heights), dims[dim] // shards_of).reshape((-1,) + (1,) * (len(dims) - 1 - dim))
    return level


def profile(count, total, limit, slope):
    loads = [(1 << 20) // math.isqrt(rank ** slope) + 1 for rank in range(2, count + 1)]
    surplus, given = total - limit - (count - 1), [1] * (count - 1)
    while surplus > 0:
        movable = [i for i in range(count - 1) if given[i] < limit]
        whole, budget = sum([loads[i] for i in movable]), surplus
        for i in movable:
            more = min(limit - given[i], max(1, budget * loads[i] // whole), surplus)
            given[i] = given[i] + more
            surplus = surplus - more
    return np.array([limit] + given)


def uneven_parts(key, amount, total, bound, skew):
    if amount == 2:
        one = jax.random.randint(key, (), max(1, total - bound), min(bound, total - 1) + 1)
        return jnp.stack([one, total - one])
    lengths = jnp.asarray(profile(amount, total, bound, skew), jnp.int32)
    pairs = (amount - 1) // 2
    giver, taker = lengths[1:1 + 2 * pairs:2], lengths[2:2 + 2 * pairs:2]
    margin = jnp.minimum(giver - 1, bound - taker)
    shifted = jax.random.randint(jax.random.fold_in(key, 1), (pairs,), 0, 1 << 20) % (margin + 1)
    lengths = lengths.at[1:1 + 2 * pairs:2].set(giver - shifted).at[2:2 + 2 * pairs:2].set(taker + shifted)
    return lengths[jax.random.permutation(jax.random.fold_in(key, 2), amount)]


def noise(own_key, dims, scale, bound, pieces=(), held_as=jnp.bfloat16):
    values = scale * jax.random.normal(own_key, dims, jnp.float32)
    if pieces:
        values = values * block_scale(own_key, dims, pieces, -0.22, 0.18)
    return jnp.clip(values, -bound, bound).astype(held_as)


def setup_inputs(seed: int = 0) -> dict:
    seeds = jax.random.split(jax.random.key(seed), 27)
    x_prefix = noise(seeds[0], (TOK_PREFIX, DP), 1.0, 6.0, ((0, 32),))
    x_action = noise(seeds[1], (TOK_ACTION, DA), 1.0, 6.0, ((0, 32),))
    cot_prefix = noise(seeds[2], (TOK_PREFIX, DP), 1.0, 6.0, ((0, 32),))
    cot_action = noise(seeds[3], (TOK_ACTION, DA), 1.0, 6.0, ((0, 32),))
    prefix_block = jax.vmap(lambda own: jnp.searchsorted(jnp.cumsum(uneven_parts(own, PREFIX_BLOCKS, PRE, PRE // 2, 0)), jnp.arange(PRE), side="right"))(jax.random.split(seeds[4], N_WIDE)).reshape((N_WIDE, PRE)).astype(jnp.int32)
    action_block = jax.vmap(lambda own: jnp.searchsorted(jnp.cumsum(uneven_parts(own, 2, ACT, ACT - 1, 0)), jnp.arange(ACT), side="right"))(jax.random.split(seeds[5], N_WIDE)).reshape((N_WIDE, ACT)).astype(jnp.int32)
    valid_len = touch_ends(jax.random.randint(seeds[6], (N_WIDE,), PRE // 2, PRE + 1), jax.random.fold_in(seeds[6], 1), PRE // 2, PRE).astype(jnp.int32)
    mix_weight = jnp.clip(jnp.exp(math.log(4.0) - 2.7725887 * jax.random.uniform(seeds[7], (N_WIDE,), jnp.float32) ** block_scale(seeds[7], (N_WIDE,), ((0, 8),), -0.2, 0.2)), 0.25, 4.0)
    wq_prefix = noise(seeds[8], (DP, HEADS * HD), DP ** -0.5, 0.125, ((0, 8), (1, 4)))
    wk_prefix = noise(seeds[9], (DP, HD), DP ** -0.5, 0.125, ((0, 32),))
    wv_prefix = noise(seeds[10], (DP, HD), DP ** -0.5, 0.125, ((0, 32),))
    wo_prefix = noise(seeds[11], (HEADS * HD, DP), (max(HEADS * HD // 256, 1)) ** -0.5, 2.0, ((0, 4), (1, 8)))
    wg_prefix = noise(seeds[12], (DP, FFP), DP ** -0.5, 0.125, ((0, 8), (1, 4)))
    wu_prefix = noise(seeds[13], (DP, FFP), DP ** -0.5, 0.125, ((0, 8), (1, 4)))
    wd_prefix = noise(seeds[14], (FFP, DP), FFP ** -0.5, 0.046875, ((0, 4), (1, 8)))
    norm1_prefix = jnp.clip(1.0 + 0.18 * jax.random.normal(seeds[15], (DP,), jnp.float32), 0.099609375, 1.8984375).astype(jnp.bfloat16)
    norm2_prefix = jnp.clip(1.0 + 0.18 * jax.random.normal(seeds[16], (DP,), jnp.float32), 0.099609375, 1.8984375).astype(jnp.bfloat16)
    wq_action = noise(seeds[17], (DA, HEADS * HD), DA ** -0.5, 0.1875, ((0, 8), (1, 4)))
    wk_action = noise(seeds[18], (DA, HD), DA ** -0.5, 0.1875, ((0, 32),))
    wv_action = noise(seeds[19], (DA, HD), DA ** -0.5, 0.1875, ((0, 32),))
    wo_action = noise(seeds[20], (HEADS * HD, DA), (max(HEADS * HD // 256, 1)) ** -0.5, 2.0, ((0, 4), (1, 8)))
    wg_action = noise(seeds[21], (DA, FFA), DA ** -0.5, 0.1875, ((0, 8), (1, 4)))
    wu_action = noise(seeds[22], (DA, FFA), DA ** -0.5, 0.1875, ((0, 8), (1, 4)))
    wd_action = noise(seeds[23], (FFA, DA), FFA ** -0.5, 0.09375, ((0, 4), (1, 8)))
    norm1_action = jnp.clip(1.0 + 0.18 * jax.random.normal(seeds[24], (DA,), jnp.float32), 0.099609375, 1.8984375).astype(jnp.bfloat16)
    norm2_action = jnp.clip(1.0 + 0.18 * jax.random.normal(seeds[25], (DA,), jnp.float32), 0.099609375, 1.8984375).astype(jnp.bfloat16)
    return dict(x_prefix=x_prefix, x_action=x_action, cot_prefix=cot_prefix, cot_action=cot_action, prefix_block=prefix_block, action_block=action_block, valid_len=valid_len, mix_weight=mix_weight, wq_prefix=wq_prefix, wk_prefix=wk_prefix, wv_prefix=wv_prefix, wo_prefix=wo_prefix, wg_prefix=wg_prefix, wu_prefix=wu_prefix, wd_prefix=wd_prefix, norm1_prefix=norm1_prefix, norm2_prefix=norm2_prefix, wq_action=wq_action, wk_action=wk_action, wv_action=wv_action, wo_action=wo_action, wg_action=wg_action, wu_action=wu_action, wd_action=wd_action, norm1_action=norm1_action, norm2_action=norm2_action)


@jax.custom_vjp
def low(v):
    return lax.optimization_barrier(v.astype(jnp.bfloat16)).astype(jnp.float32)

@jax.custom_vjp
def low_back(v):
    return v

def low_keep(v):
    return (low(v), None)

def low_pass(kept, grad):
    return (grad,)

def back_keep(v):
    return (v, None)

def back_low(kept, grad):
    return (low(grad),)
low.defvjp(low_keep, low_pass)
low_back.defvjp(back_keep, back_low)
epsilon = 1e-06
scaling = 0.0625
masked_score = -1e+30

def product(former, latter):
    return jnp.dot(former, latter, precision=lax.Precision.HIGHEST, preferred_element_type=jnp.float32)

def rms_norm(features, weight):
    return features * lax.rsqrt(lax.optimization_barrier(jnp.mean(features * features, axis=-1, keepdims=True)) + epsilon) * weight

def stream_open(features, weight, query_proj, key_proj, value_proj):
    normed = low(rms_norm(features, weight))
    query = low_back(low(product(normed, query_proj) * scaling))
    key_rows = low_back(low(product(normed, key_proj)))
    value_rows = low_back(low(product(normed, value_proj)))
    return (query, key_rows, value_rows)

def stream_close(features, mixed_rows, weight, out_proj, gate_proj, up_proj, down_proj):
    attended = low_back(product(mixed_rows, out_proj))
    middle = features + attended
    normed = low(rms_norm(middle, weight))
    gate_rows = low_back(product(normed, gate_proj))
    uppers = low_back(product(normed, up_proj))
    hidden = low(jax.nn.gelu(gate_rows, approximate=True) * uppers)
    return middle + low_back(product(hidden, down_proj))

def attend(query, key_rows, value_rows, allowed):
    count = query.shape[0]
    headed = query.reshape(count, HEADS, HD)
    scores = low_back(jnp.einsum('qhd,kd->hqk', headed, key_rows, precision=lax.Precision.HIGHEST))
    scores = jnp.where(allowed[None], scores, masked_score)
    highest = lax.optimization_barrier(jnp.max(scores, axis=-1, keepdims=True))
    exponent = jnp.exp(scores - highest)
    attention = low(exponent / lax.optimization_barrier(jnp.sum(exponent, axis=-1, keepdims=True)))
    mixed_rows = jnp.einsum('hqk,kd->qhd', attention, value_rows, precision=lax.Precision.HIGHEST)
    return low_back(low(mixed_rows.reshape(count, HEADS * HD)))

def item_forward(weights, item):
    prefix_rows, action_rows, block_prefix, block_action, length = item
    prefix_set = weights[:9]
    action_set = weights[9:]
    query_p, key_p, value_p = stream_open(prefix_rows, prefix_set[7], prefix_set[0], prefix_set[1], prefix_set[2])
    query_a, key_a, value_a = stream_open(action_rows, action_set[7], action_set[0], action_set[1], action_set[2])
    blocks = jnp.concatenate([block_prefix, block_action + PREFIX_BLOCKS]).astype(jnp.int32)
    usable = jnp.concatenate([jnp.arange(PRE, dtype=jnp.int32) < length, jnp.ones((ACT,), dtype=jnp.bool_)])
    allowed = (blocks[None, :] <= blocks[:, None]) & usable[None, :]
    mixed_rows = attend(jnp.concatenate([query_p, query_a], axis=0), jnp.concatenate([key_p, key_a], axis=0), jnp.concatenate([value_p, value_a], axis=0), allowed)
    out_p = stream_close(prefix_rows, mixed_rows[:PRE], prefix_set[8], prefix_set[3], prefix_set[4], prefix_set[5], prefix_set[6])
    out_a = stream_close(action_rows, mixed_rows[PRE:], action_set[8], action_set[3], action_set[4], action_set[5], action_set[6])
    return (out_p, out_a)

def reference(x_prefix, x_action, cot_prefix, cot_action, prefix_block, action_block, valid_len, mix_weight, wq_prefix, wk_prefix, wv_prefix, wo_prefix, wg_prefix, wu_prefix, wd_prefix, norm1_prefix, norm2_prefix, wq_action, wk_action, wv_action, wo_action, wg_action, wu_action, wd_action, norm1_action, norm2_action):
    weights = tuple((matrix.astype(jnp.float32) for matrix in (wq_prefix, wk_prefix, wv_prefix, wo_prefix, wg_prefix, wu_prefix, wd_prefix, norm1_prefix, norm2_prefix, wq_action, wk_action, wv_action, wo_action, wg_action, wu_action, wd_action, norm1_action, norm2_action)))
    prefix_rows = x_prefix.astype(jnp.float32).reshape(N_WIDE, PRE, DP)
    action_rows = x_action.astype(jnp.float32).reshape(N_WIDE, ACT, DA)

    def forward(weights, prefix_rows, action_rows):

        def one_item(item):
            return item_forward(weights, item)
        return lax.map(jax.checkpoint(one_item), (prefix_rows, action_rows, prefix_block, action_block, valid_len))
    outs, pullback = jax.vjp(forward, weights, prefix_rows, action_rows)
    cot_p = cot_prefix.astype(jnp.float32).reshape(N_WIDE, PRE, DP) * mix_weight[:, None, None]
    cot_a = cot_action.astype(jnp.float32).reshape(N_WIDE, ACT, DA) * mix_weight[:, None, None]
    grads, grad_p, grad_a = pullback((cot_p, cot_a))
    return (outs[0].astype(jnp.bfloat16).reshape(TOK_PREFIX, DP), outs[1].astype(jnp.bfloat16).reshape(TOK_ACTION, DA), grad_p.reshape(TOK_PREFIX, DP), grad_a.reshape(TOK_ACTION, DA), grads[0], grads[1], grads[2], grads[3], grads[4], grads[5], grads[6], grads[7], grads[8], grads[9], grads[10], grads[11], grads[12], grads[13], grads[14], grads[15], grads[16], grads[17])
```

```python
import functools

import jax
import jax.numpy as jnp
from jax import lax
from jax.experimental import pallas as pl
from jax.experimental.pallas import tpu as pltpu
from jax.sharding import PartitionSpec as P

PREFIX_BLOCKS = 4
BOTH = ("wide", "narrow")

epsilon = 1e-06
scaling = 0.0625
masked_score = -1e30
low = jnp.bfloat16
wider = jnp.float32


def rms_norm(features, weight):
    return (
        features
        * lax.rsqrt(jnp.mean(features * features, axis=-1, keepdims=True) + epsilon)
        * weight
    )


def product(former, latter):
    return jnp.dot(former, latter, preferred_element_type=wider)


def rows_contract(former, latter):
    return lax.dot_general(
        former, latter, (((0,), (0,)), ((), ())), preferred_element_type=wider
    )


def cols_contract(former, latter):
    return lax.dot_general(
        former, latter, (((1,), (1,)), ((), ())), preferred_element_type=wider
    )


def norm_back(features, weight, upstream):
    unused, pullback = jax.vjp(rms_norm, features, weight)
    return pullback(upstream)


def tie(value, *earlier):
    return lax.optimization_barrier((value, *earlier))[0] if earlier else value


def masked_scores(queries, key_rows, allowed):
    scores = jnp.einsum("qhd,kd->hqk", queries, key_rows, preferred_element_type=wider)
    return jnp.where(allowed[None], scores, masked_score)


def copies_kernel(plan, n_in, place_ref, *refs):
    copied = refs[-1]
    copies = []
    for i, (source, source_at, target, target_at) in enumerate(plan):
        source_ref = refs[source].at[source_at(place_ref)]
        target_ref = refs[n_in + target].at[target_at(place_ref)]
        copies.append(pltpu.make_async_copy(source_ref, target_ref, copied.at[i]))
    for copy in copies:
        copy.start()
    for copy in copies:
        copy.wait()


def copy_blocks(plan, places, arrays, shapes, name):
    any_spec = pl.BlockSpec(memory_space=pl.ANY)
    moved = 2 * sum(shape[0] * shape[1] * 2 for shape in shapes)
    return pl.pallas_call(
        functools.partial(copies_kernel, plan, len(arrays)),
        in_specs=[pl.BlockSpec(memory_space=pltpu.SMEM)] + [any_spec] * len(arrays),
        out_specs=[pl.BlockSpec(memory_space=pltpu.VMEM)] * len(shapes),
        scratch_shapes=[pltpu.SemaphoreType.DMA((len(plan),))],
        compiler_params=pltpu.CompilerParams(vmem_limit_bytes=24 << 20),
        out_shape=[jax.ShapeDtypeStruct(shape, low) for shape in shapes],
        cost_estimate=pl.CostEstimate(flops=0, bytes_accessed=moved, transcendentals=0),
        name=name,
    )(places, *arrays)


def block(index, size):
    return pl.ds(pl.multiple_of(index * size, size), size)


def feed_kernel(count, half, n_kept, n_copied, first, *refs):
    token_refs, refs = refs[:count], refs[count:]
    grad_refs, refs = refs[:count], refs[count:]
    weight_refs, refs = refs[:4], refs[4 + n_kept :]
    kept_refs, row_refs = refs[:n_copied], refs[n_copied : n_copied + 4]
    back_ref, out_ref, copied = refs[n_copied + 4 :]
    step = pl.program_id(0)
    tile = token_refs[0].shape[0]
    width = weight_refs[1].shape[1]
    columns_of = (slice(0, width), slice(width, width + weight_refs[3].shape[1]))
    slope = 0.7978845608028654

    def run(token_ref, grad_ref):
        place = block(first + step, tile)
        copies = [
            pltpu.make_async_copy(
                source.at[:, columns_of[i % 2]], kept_refs[i].at[place], copied.at[i]
            )
            for i, source in enumerate((token_ref, token_ref, grad_ref, grad_ref)[:n_copied])
        ]
        for copy in copies:
            copy.start()
        for i, columns in enumerate(columns_of):
            gate_up_ref, down_ref = weight_refs[2 * i : 2 * i + 2]
            hidden_ref, both_ref = row_refs[2 * i : 2 * i + 2]
            units = down_ref.shape[0]
            both = product(token_ref[:, columns], gate_up_ref[...])
            gate, up = both[:, :units], both[:, units:]
            square = gate * gate
            bend = jnp.tanh(slope * gate * (1.0 + 0.044715 * square))
            active = 0.5 * gate * (1.0 + bend)
            hidden = (active * up).astype(low)
            hidden_ref[...] = hidden
            dhidden = cols_contract(grad_ref[:, columns], down_ref[...])
            steep = 0.5 * (1.0 + bend) + 0.5 * gate * (1.0 - bend * bend) * slope * (
                1.0 + 3 * 0.044715 * square
            )
            both_ref[:, :units] = (dhidden * up * steep).astype(low)
            both_ref[:, units:] = (dhidden * active).astype(low)
            back_ref[:, columns] = cols_contract(both_ref[...], gate_up_ref[...]).astype(low)
            out_ref[:, columns] = product(hidden, down_ref[...]).astype(low)
        for copy in copies:
            copy.wait()

    for piece in range(count):
        pl.when(step // half == piece)(
            functools.partial(run, token_refs[piece], grad_refs[piece])
        )


def feed_forward(tokens, grads, weights, kept, size, total, first, n_copied):
    count = len(tokens)
    columns = tokens[0][0].shape[1]
    tile = min(size, 256)
    half = size // tile
    units = [weights[1].shape[0], weights[3].shape[0]]
    widths = [weights[1].shape[1], weights[3].shape[1]]
    first = first * half
    rows = [units[0], 2 * units[0], units[1], 2 * units[1]]
    any_spec = pl.BlockSpec(memory_space=pl.ANY)

    def piece_spec(piece, place):
        return pl.BlockSpec(
            (tile, columns),
            lambda i: (place * half + jnp.clip(i - piece * half, 0, half - 1), 0),
        )

    out = pl.pallas_call(
        functools.partial(feed_kernel, count, half, len(kept), n_copied, first),
        grid=(count * half,),
        in_specs=[piece_spec(i, place) for i, (unused, place) in enumerate(tokens)]
        + [piece_spec(i, place) for i, (unused, place) in enumerate(grads)]
        + [
            pl.BlockSpec(w.shape, lambda i: (0, 0), pipeline_mode=pl.Buffered(1)) for w in weights
        ]
        + [any_spec] * len(kept),
        out_specs=[any_spec] * n_copied
        + [pl.BlockSpec((tile, w), lambda i: (first + i, 0)) for w in rows]
        + [pl.BlockSpec((tile, columns), lambda i: (i, 0))] * 2,
        scratch_shapes=[pltpu.SemaphoreType.DMA((4,))],
        out_shape=[
            jax.ShapeDtypeStruct((total, w), low) for w in (widths * 2)[:n_copied] + rows
        ]
        + [jax.ShapeDtypeStruct((count * size, columns), low)] * 2,
        input_output_aliases={2 * count + 4 + i: i for i in range(len(kept))},
        compiler_params=pltpu.CompilerParams(vmem_limit_bytes=52 << 20),
        cost_estimate=pl.CostEstimate(
            flops=2 * count * size * 6 * (widths[0] * units[0] + widths[1] * units[1]),
            bytes_accessed=12 * count * size * columns,
            transcendentals=0,
        ),
        name="feed_forward",
    )(*(array for array, unused in tokens), *(array for array, unused in grads), *weights, *kept)
    return out[: n_copied + 4], out[n_copied + 4], out[n_copied + 5]


def make_local(n_wide, n_narrow):
    n_all = n_wide * n_narrow
    wide_masks = [1 << bit for bit in range(n_wide.bit_length() - 1)]
    far = [("wide", mask) for mask in wide_masks[:0:-1]]
    side, across, core = ("wide", 1), ("narrow", 2), ("narrow", 1)
    sizes = {"wide": n_wide, "narrow": n_narrow}

    def join(*values):
        return lax.optimization_barrier(values)

    def hop(value, link, *earlier):
        axis, mask = link
        value = tie(value, *earlier)
        return lax.ppermute(value, axis, [(i, i ^ mask) for i in range(sizes[axis])])

    def rank_of(link):
        return link[1] if link[0] == "narrow" else link[1] * n_narrow

    def gather_blocks(block, links, at, events, *earlier):
        held = []
        for i, link in enumerate(links):
            position = sum(other > rank_of(link) for other in held)
            moved = hop(block, link, *(earlier[i] if i < len(earlier) else ()))
            events.append(moved)
            block = jnp.where(
                (at[link[0]] & link[1]) != 0,
                jnp.stack([moved, block], position),
                jnp.stack([block, moved], position),
            )
            held.append(rank_of(link))
        return block.reshape(-1, *block.shape[len(links) :])

    def scatter_blocks(blocks, links, at, events=None, earlier=()):
        held = sorted((rank_of(link) for link in links), reverse=True)
        blocks = blocks.reshape(*(2 for unused in links), *blocks.shape[1:])
        for stage, link in enumerate(links):
            position = held.index(rank_of(link))
            bit = jnp.minimum(at[link[0]] & link[1], 1)
            mine = lax.dynamic_index_in_dim(blocks, bit, position, keepdims=False)
            theirs = lax.dynamic_index_in_dim(blocks, 1 - bit, position, keepdims=False)
            moved = hop(theirs, link, *at_stage(earlier, stage))
            if events is not None:
                events.append(moved)
            blocks = mine.astype(wider) + moved.astype(wider)
            if stage + 1 < len(links):
                blocks = blocks.astype(low)
            held.remove(rank_of(link))
        return blocks

    def at_stage(earlier, stage):
        return earlier[stage] if stage < len(earlier) else ()

    def gather_rows(rows, links, events, earlier=()):
        for stage, link in enumerate(links):
            moved = hop(rows, link, *at_stage(earlier, stage))
            events.append(moved)
            rows = jnp.concatenate([rows, moved], axis=0)
        return rows

    def scatter_rows(rows, links, events, earlier=()):
        for stage, link in enumerate(links):
            half = rows.shape[0] // 2
            moved = hop(rows[half:], link, *at_stage(earlier, stage))
            events.append(moved)
            rows = rows[:half].astype(wider) + moved.astype(wider)
            if stage + 1 < len(links):
                rows = rows.astype(low)
        return rows

    def gather_all(rows, events, even, earlier=()):
        own = gather_rows(rows, far, events, earlier)
        sides, last = at_stage(earlier, len(far)), at_stage(earlier, len(far) + 1)
        from_x, from_y = hop(own, across, *sides), hop(own, side, *sides)
        events.append(from_y)
        half = own.shape[0] // 2
        if even:
            corner = jnp.concatenate(
                [hop(from_y[:half], across, *last), hop(from_x[half:], side, *last)], axis=0
            )
        else:
            corner = hop(from_y, across, *last)
        return own, from_x, from_y, corner

    def scatter_all(most, other_most, corner, other_corner, events, even, earlier=()):
        chip, first, second = (at_stage(earlier, stage) for stage in range(3))
        corner = corner.astype(wider) + hop(other_corner, core, *chip).astype(wider)
        corner = corner.astype(low)
        size = corner.shape[0]
        half = size // 2 if even else size
        for_y = hop(corner[:half], across, *first)
        events.append(for_y)
        sums = []
        for i in range(3):
            rows = slice(i * size, (i + 1) * size)
            moved = other_most[i] if isinstance(other_most, list) else other_most[rows]
            sums.append((most[rows], moved))
        own, sum_x, sum_y = (mine.astype(wider) + moved.astype(wider) for mine, moved in sums)
        if even:
            for_x = hop(corner[half:], side, *first)
            sum_x = jnp.concatenate([sum_x[:half], sum_x[half:] + for_x.astype(wider)], axis=0)
            sum_y = jnp.concatenate([sum_y[:half] + for_y.astype(wider), sum_y[half:]], axis=0)
        else:
            sum_y = sum_y + for_y.astype(wider)
        moved_x = hop(sum_x.astype(low), across, *second)
        moved_y = hop(sum_y.astype(low), side, *second)
        events.append(moved_y)
        total = own + moved_x.astype(wider) + moved_y.astype(wider)
        return scatter_rows(total.astype(low), far[::-1], events, earlier[3:])

    def local(
        x_prefix,
        x_action,
        cot_prefix,
        cot_action,
        prefix_block,
        action_block,
        valid_len,
        mix_weight,
        wq_prefix,
        wk_prefix,
        wv_prefix,
        wo_prefix,
        wg_prefix,
        wu_prefix,
        wd_prefix,
        norm1_prefix,
        norm2_prefix,
        wq_action,
        wk_action,
        wv_action,
        wo_action,
        wg_action,
        wu_action,
        wd_action,
        norm1_action,
        norm2_action,
    ):
        at = {"wide": lax.axis_index("wide"), "narrow": lax.axis_index("narrow")}
        head_dim = wk_prefix.shape[1]
        own = x_prefix.shape[0]
        width = x_prefix.shape[1]

        def streams(packed):
            return [packed[:, :width], packed[:, width:]]

        depth = [wg_prefix.shape[0], wg_action.shape[0]]
        units = [wg_prefix.shape[1] // n_wide, wg_action.shape[1] // n_wide]

        def fold(rows, lead):
            return jnp.concatenate(
                [rows[i * lead : (i + 1) * lead] for i in range(rows.shape[0] // lead)], axis=1
            )

        def unfold(rows, columns):
            return jnp.concatenate(
                [
                    rows[:, i * columns : (i + 1) * columns]
                    for i in range(rows.shape[1] // columns)
                ],
                axis=0,
            )

        def pack(parts):
            gate_p, up_p, down_p, gate_a, up_a, down_a = parts
            action = jnp.concatenate([gate_a, up_a, fold(down_a, depth[1])], axis=1)
            action = jnp.pad(action, [(0, 0), (0, units[0] - action.shape[1])])
            return jnp.concatenate([gate_p, up_p, fold(down_p, depth[0]), action], axis=0)

        def unpack(packet):
            d, f = depth[0], units[1]
            action = packet[3 * d :]
            return (
                packet[:d],
                packet[d : 2 * d],
                unfold(packet[2 * d : 3 * d], d),
                action[:, :f],
                action[:, f : 2 * f],
                unfold(action[:, 2 * f : 3 * f], depth[1]),
            )

        distances = list(range(1, n_wide))

        aligned = units[1] % 128 == 0 and depth[1] % 16 == 0 and units[1] == depth[1]
        folds = units[0] // depth[0]
        packet_shape = (3 * depth[0] + depth[1], units[0])
        peers = at["wide"] ^ jnp.arange(n_wide, dtype=jnp.int32)

        copying = n_all * own <= 4096

        def packet_plan(outward, blocks_of):
            plan = []
            for k in range(n_wide):
                for array, array_at, packet_at in blocks_of(k):
                    if outward:
                        plan.append((array, array_at, k, lambda ref, at=packet_at: at))
                    else:
                        plan.append((k, lambda ref, at=packet_at: at, array, array_at))
            return plan

        def span(start, size):
            return slice(start, start + size)

        def packet_places(k, gate_at, up_at, down_at, arrays):
            for i, (d, f) in enumerate(zip(depth, units, strict=True)):
                gate, up, down = arrays[3 * i : 3 * i + 3]
                top = 3 * depth[0] if i else 0
                second = (span(top, d), span(f, f)) if i else (span(d, d), span(0, f))
                yield gate, functools.partial(gate_at, k, d, f), (span(top, d), span(0, f))
                yield up, functools.partial(up_at, k, d, f), second
                for part in range(f // d):
                    place = (span(top, d), span(2 * f, d)) if i else (span(2 * d, d), span(part * d, d))
                    yield down, functools.partial(down_at, k, d, f, part), place

        def weight_packet(k):
            peer = at["wide"] ^ k
            f, g = units
            return pack(
                (
                    lax.dynamic_slice_in_dim(wg_prefix, peer * f, f, 1),
                    lax.dynamic_slice_in_dim(wu_prefix, peer * f, f, 1),
                    lax.dynamic_slice_in_dim(wd_prefix, peer * f, f, 0),
                    lax.dynamic_slice_in_dim(wg_action, peer * g, g, 1),
                    lax.dynamic_slice_in_dim(wu_action, peer * g, g, 1),
                    lax.dynamic_slice_in_dim(wd_action, peer * g, g, 0),
                )
            )

        if aligned:
            packets = copy_blocks(
                packet_plan(
                    True,
                    lambda k: packet_places(
                        k,
                        lambda k, d, f, ref: (slice(None), block(ref[k], f)),
                        lambda k, d, f, ref: (slice(None), block(ref[k], f)),
                        lambda k, d, f, part, ref: (
                            pl.ds(pl.multiple_of(ref[k] * f, f) + part * d, d),
                            slice(None),
                        ),
                        range(6),
                    ),
                ),
                peers,
                [wg_prefix, wu_prefix, wd_prefix, wg_action, wu_action, wd_action],
                [packet_shape] * n_wide,
                "pack_weights",
            )
            packets = dict(enumerate(packets))
            weight_packet = packets.get
        else:
            packets = {0: weight_packet(0)}

        def send_packets(few, packet_of, *earlier):
            for k in few:
                packets[k] = hop(packet_of(k), ("wide", k), *earlier)

        def share(first, last):
            return [k for k in distances if first * n_wide <= 8 * k < last * n_wide]

        narrow_links = [across, core]
        x_packed = jnp.concatenate([x_prefix, x_action], axis=1)
        item_packed = gather_rows(x_packed, narrow_links, [])
        item_rows = streams(item_packed)

        gain_parts = [norm1_prefix, norm2_prefix, norm1_action, norm2_action]
        gain_sizes = [part.shape[0] for part in gain_parts]
        gain_stops = [sum(gain_sizes[: i + 1]) for i in range(4)]
        keyval_rows_of = [wk_prefix.shape[0], wk_action.shape[0]]
        gain_start = sum(keyval_rows_of)
        gain_rows = 16

        def pad_gains(row):
            return jnp.pad(
                row[..., None, :],
                [(0, 0)] * (row.ndim - 1) + [(0, gain_rows - 1), (0, 2 * head_dim - row.shape[-1])],
            )

        shared_events, query_events, out_events = [], [], []
        query_depth = [wq_prefix.shape[0], wq_action.shape[0]]
        query_half = wq_prefix.shape[1] // 2
        query_packed = jnp.concatenate([wq_prefix, wq_action], axis=0)
        wide_links = far + [side]
        query_blocks = [
            gather_blocks(query_packed[:, :query_half], wide_links, at, []),
            gather_blocks(
                query_packed[:, query_half:],
                [side] + far,
                at,
                query_events,
                (),
                (packets[max(packets)],),
            ),
        ]
        send_packets(share(4, 5), weight_packet, query_events[0])
        shared = gather_blocks(
            jnp.concatenate(
                [
                    jnp.concatenate([wk_prefix, wv_prefix], axis=1),
                    jnp.concatenate([wk_action, wv_action], axis=1),
                    pad_gains(jnp.concatenate(gain_parts)),
                ],
                axis=0,
            ),
            far + [side, across, core],
            at,
            shared_events,
            *[()] * (len(far) + 2),
            tuple(packets[k] for k in share(4, 5)),
        )
        send_packets(share(5, 6), weight_packet, shared_events[-2])
        send_packets(share(0, 2), weight_packet, shared_events[-2])
        gains_all = shared[:, gain_start, :].astype(wider)
        gains = [
            gains_all[:, stop - size : stop].reshape(-1)
            for stop, size in zip(gain_stops, gain_sizes, strict=True)
        ]
        first_gain = [gains[0], gains[2]]
        second_gain = [gains[1], gains[3]]
        keyval_weight = [
            shared[:, : keyval_rows_of[0]].reshape(-1, 2 * head_dim),
            shared[:, keyval_rows_of[0] : gain_start].reshape(-1, 2 * head_dim),
        ]
        query_weight = [
            [blocks[:, : query_depth[0]].reshape(-1, query_half) for blocks in query_blocks],
            [blocks[:, query_depth[0] :].reshape(-1, query_half) for blocks in query_blocks],
        ]
        out_held = gather_blocks(
            jnp.concatenate([wo_prefix.T, wo_action.T], axis=0),
            far,
            at,
            out_events,
            (query_events[1],),
        )
        out_moved = hop(out_held.reshape(*(2 for unused in far), *out_held.shape[1:]), side)
        item_weight = mix_weight[0]
        dout = jnp.concatenate([cot_prefix, cot_action], axis=1).astype(wider) * item_weight

        all_normed = [
            rms_norm(item_rows[stream].astype(wider), first_gain[stream]).astype(low)
            for stream in range(2)
        ]
        prefix_len = item_packed.shape[0]
        total_rows = 2 * prefix_len
        joined = jnp.concatenate(
            [
                product(all_normed[stream], keyval_weight[stream]).astype(low)
                for stream in range(2)
            ],
            axis=0,
        )
        key_rows = joined[:, :head_dim]
        values = joined[:, head_dim:]
        queries = jnp.concatenate(
            [
                jnp.concatenate(
                    [
                        (product(all_normed[stream], part) * scaling).astype(low)
                        for part in query_weight[stream]
                    ],
                    axis=1,
                )
                for stream in range(2)
            ],
            axis=0,
        ).reshape(total_rows, -1, head_dim)
        offsets = [0]
        for unused, mask in narrow_links:
            offsets = offsets + [offset ^ mask for offset in offsets]
        owners = at["narrow"] ^ jnp.array(offsets, jnp.int32)

        def reorder(ids):
            return jnp.take(ids.reshape(n_narrow, -1), owners, axis=0).reshape(-1)

        blocks = jnp.concatenate(
            [reorder(prefix_block[0]), reorder(action_block[0]) + PREFIX_BLOCKS]
        )
        positions = (owners[:, None] * own + jnp.arange(own, dtype=jnp.int32)[None]).reshape(-1)
        usable = jnp.concatenate(
            [
                positions < valid_len[0],
                jnp.ones((total_rows - prefix_len,), dtype=jnp.bool_),
            ]
        )
        allowed = (blocks[None, :] <= blocks[:, None]) & usable[None, :]
        scores = masked_scores(queries, key_rows, allowed)
        highest = jnp.max(scores, axis=-1, keepdims=True)
        exponent = jnp.exp(scores - highest)
        denominator = jnp.sum(exponent, axis=-1, keepdims=True)
        log_total = highest + jnp.log(denominator)
        attention = (exponent / denominator).astype(low)
        mixed_all = jnp.einsum("hqk,kd->qhd", attention, values, preferred_element_type=wider)
        mixed_all = mixed_all.astype(low).reshape(total_rows, -1)
        mixed_rows = [mixed_all[:prefix_len], mixed_all[prefix_len:]]
        out_moved, mixed_all = join(out_moved, mixed_all)
        mixed_rows = [mixed_all[:prefix_len], mixed_all[prefix_len:]]
        out_held = out_held.reshape(out_moved.shape)
        out_blocks = jnp.where(
            (at["wide"] & 1) != 0,
            jnp.stack([out_moved, out_held], len(far)),
            jnp.stack([out_held, out_moved], len(far)),
        )
        out_blocks = out_blocks.reshape(-1, *out_blocks.shape[len(far) + 1 :])
        out_weight = [
            out_blocks[:, : query_depth[0]].reshape(-1, wo_prefix.shape[0]),
            out_blocks[:, query_depth[0] :].reshape(-1, wo_action.shape[0]),
        ]
        attended_all = (
            jnp.concatenate(
                [
                    cols_contract(mixed_rows[stream], out_weight[stream]).astype(low)
                    for stream in range(2)
                ],
                axis=1,
            )
        )
        attended_events = []
        attended = scatter_rows(
            attended_all,
            [core, across],
            attended_events,
            [(), tuple(packets[k] for k in share(5, 6))],
        )
        send_packets(share(7, 8), weight_packet, attended_events[1])
        send_packets(share(3, 4), weight_packet, attended_events[1])
        inputs = [x_prefix.astype(wider), x_action.astype(wider)]
        middle = [
            rows + part for rows, part in zip(inputs, streams(attended), strict=True)
        ]
        normed2 = jnp.concatenate(
            [rms_norm(middle[stream], second_gain[stream]).astype(low) for stream in range(2)],
            axis=1,
        )
        token_events = []
        near = gather_all(
            normed2,
            token_events,
            True,
            [tuple(packets[k] for k in share(0, 2))]
            + [()] * (len(far) - 1)
            + [
                tuple(packets[k] for k in share(7, 8)),
                tuple(packets[k] for k in share(3, 4)),
            ],
        )
        send_packets(share(6, 7), weight_packet, token_events[-2])
        send_packets(share(2, 3), weight_packet, token_events[-2])
        grad_near = gather_all(
            dout.astype(low),
            [],
            False,
            [(shared_events[-3],)]
            + [(shared_events[-1],)] * (len(far) - 1)
            + [(attended_events[0],), (token_events[-2],)],
        )
        if aligned:
            feed_weights = copy_blocks(
                packet_plan(
                    False,
                    lambda k: packet_places(
                        k,
                        lambda k, d, f, ref: (block(ref[k], d), span(0, f)),
                        lambda k, d, f, ref: (block(ref[k], d), span(f, f)),
                        lambda k, d, f, part, ref: (span(part * d, d), block(ref[k], d)),
                        (0, 0, 1, 2, 2, 3),
                    ),
                ),
                peers,
                [packets[k] for k in range(n_wide)],
                [
                    (depth[0] * n_wide, 2 * units[0]),
                    (units[0], depth[0] * n_wide),
                    (depth[1] * n_wide, 2 * units[1]),
                    (units[1], depth[1] * n_wide),
                ],
                "unpack_weights",
            )
        else:
            gate_up_weight = [jnp.zeros((depth[i] * n_wide, 2 * units[i]), low) for i in range(2)]
            down_weight = [jnp.zeros((units[i], depth[i] * n_wide), low) for i in range(2)]
            for k, packet in packets.items():
                peer = at["wide"] ^ k
                parts = unpack(packet)
                for i in range(2):
                    gate_up_weight[i] = lax.dynamic_update_slice_in_dim(
                        gate_up_weight[i],
                        jnp.concatenate(parts[3 * i : 3 * i + 2], axis=1),
                        peer * depth[i],
                        0,
                    )
                    down_weight[i] = lax.dynamic_update_slice_in_dim(
                        down_weight[i], parts[3 * i + 2], peer * depth[i], 1
                    )
            feed_weights = [gate_up_weight[0], down_weight[0], gate_up_weight[1], down_weight[1]]

        size = near[0].shape[0]
        feed = functools.partial(
            feed_forward,
            weights=feed_weights,
            size=size,
            total=n_all * own,
            n_copied=4 if copying else 0,
        )
        if copying:
            other_most = hop(jnp.concatenate(near[:3], axis=0), core)
            token_far = [(other_most, i) for i in range(3)] + [(hop(near[3], core), 0)]
            grad_near = jnp.concatenate(grad_near, axis=0)
            grad_far = hop(grad_near, core)
            grad_near, grad_far = ([(rows, i) for i in range(4)] for rows in (grad_near, grad_far))
        else:
            token_far = [(hop(rows, core), 0) for rows in near]
            grad_far = [(hop(rows, core), 0) for rows in grad_near]
            grad_near = [(rows, 0) for rows in grad_near]
        token_pieces = [(rows, 0) for rows in near] + [token_far[3], *token_far[:3]]
        grad_pieces = [*grad_near, grad_far[3], *grad_far[:3]]
        kept, back_most, out_most = feed(token_pieces[:3], grad_pieces[:3], kept=[], first=0)
        kept, back_corner, out_corner = feed(
            token_pieces[3:5], grad_pieces[3:5], kept=kept, first=3
        )
        kept, back_far, out_far = feed(token_pieces[5:], grad_pieces[5:], kept=kept, first=5)
        hidden_rows, both_rows = kept[-4::2], kept[-3::2]
        def chip_far(rows, *earlier):
            if copying:
                return hop(rows, core, *earlier)
            return [hop(rows[i * size : (i + 1) * size], core, *earlier) for i in range(3)]

        back_events = []
        dnormed2_packed = scatter_all(
            back_most,
            chip_far(back_far),
            back_corner[:size],
            back_corner[size:],
            back_events,
            True,
        )
        dnormed2 = streams(dnormed2_packed)
        if copying:
            gate_up_grad = [rows_contract(kept[i], both_rows[i]) for i in range(2)]
            down_grad = [rows_contract(hidden_rows[i], kept[2 + i]) for i in range(2)]
        else:
            gate_up_grad = [0.0, 0.0]
            down_grad = [0.0, 0.0]
            for i, ((token, token_at), (grad, grad_at)) in enumerate(
                zip(token_pieces, grad_pieces, strict=True)
            ):
                rows = slice(i * size, (i + 1) * size)
                token = streams(token[token_at * size : (token_at + 1) * size])
                grad = streams(grad[grad_at * size : (grad_at + 1) * size])
                for j in range(2):
                    gate_up_grad[j] = gate_up_grad[j] + rows_contract(token[j], both_rows[j][rows])
                    down_grad[j] = down_grad[j] + rows_contract(hidden_rows[j][rows], grad[j])
        gate_up_grad = [grad.astype(low) for grad in gate_up_grad]
        down_grad = [grad.astype(low) for grad in down_grad]

        def gradient_packet(k):
            peer = at["wide"] ^ k
            parts = []
            for i in range(2):
                both = lax.dynamic_slice_in_dim(gate_up_grad[i], peer * depth[i], depth[i], 0)
                down = lax.dynamic_slice_in_dim(down_grad[i], peer * depth[i], depth[i], 1)
                parts += [both[:, : units[i]], both[:, units[i] :], down]
            return pack(parts)

        if aligned:
            packets = copy_blocks(
                packet_plan(
                    True,
                    lambda k: packet_places(
                        k,
                        lambda k, d, f, ref: (block(ref[k], d), span(0, f)),
                        lambda k, d, f, ref: (block(ref[k], d), span(f, f)),
                        lambda k, d, f, part, ref: (span(part * d, d), block(ref[k], d)),
                        (0, 0, 1, 2, 2, 3),
                    ),
                ),
                peers,
                [gate_up_grad[0], down_grad[0], gate_up_grad[1], down_grad[1]],
                [packet_shape] * n_wide,
                "pack_gradients",
            )
            packets = dict(enumerate(packets))
            gradient_packet = packets.get
        else:
            packets = {0: gradient_packet(0)}
        send_packets(share(4, 5), gradient_packet)
        send_packets(share(2, 3), gradient_packet)
        send_packets(share(6, 7), gradient_packet, back_events[1])
        dmiddle = []
        grad_second = []
        for stream, dout_part in enumerate(streams(dout)):
            from_norm, gain_part = norm_back(middle[stream], second_gain[stream], dnormed2[stream])
            dmiddle.append(dout_part + from_norm)
            grad_second.append(gain_part)
        att_events = []
        grad_att = streams(
            gather_rows(
                jnp.concatenate([part.astype(low) for part in dmiddle], axis=1),
                narrow_links,
                att_events,
            )
        )
        send_packets(share(5, 6), gradient_packet, att_events[0])
        send_packets(share(0, 2), gradient_packet, att_events[0])
        return_events = []

        def return_wide(parts, links, events=None, earlier=()):
            blocks = jnp.concatenate(
                [part.astype(low).reshape(n_wide, -1, part.shape[1]) for part in parts], axis=1
            )
            return scatter_blocks(blocks, links, at, events, earlier)

        out_grads = return_wide(
            [rows_contract(grad_att[stream], mixed_rows[stream]) for stream in range(2)],
            wide_links[::-1],
            return_events,
        )
        send_packets(share(7, 8), gradient_packet, return_events[0])
        send_packets(share(3, 4), gradient_packet, return_events[0])
        grad_out_w = [out_grads[: query_depth[0]].T, out_grads[query_depth[0] :].T]
        dmixed = jnp.concatenate(
            [product(grad_att[stream], out_weight[stream]) for stream in range(2)],
            axis=0,
        )
        dmixed = dmixed.astype(low).reshape(total_rows, -1, head_dim)
        recomputed = jnp.exp(masked_scores(queries, key_rows, allowed) - log_total)
        dprobs = jnp.einsum("qhd,kd->hqk", dmixed, values, preferred_element_type=wider)
        row_inner = jnp.sum(recomputed * dprobs, axis=-1, keepdims=True)
        dscores = (recomputed * (dprobs - row_inner)).astype(low)
        dquery = jnp.einsum("hqk,kd->qhd", dscores, key_rows, preferred_element_type=wider)
        dquery = (dquery.astype(low) * scaling).reshape(total_rows, -1)
        grad_key = jnp.einsum("hqk,qhd->kd", dscores, queries, preferred_element_type=wider)
        dvalue = jnp.einsum(
            "hqk,qhd->kd", recomputed.astype(low), dmixed, preferred_element_type=wider
        )
        grad_keyval = jnp.concatenate([grad_key, dvalue], axis=1).astype(low)
        dquery_rows = [dquery[:prefix_len], dquery[prefix_len:]]
        keyval_rows = [grad_keyval[:prefix_len], grad_keyval[prefix_len:]]
        query_links = [[side] + far[::-1], far[::-1] + [side]]
        query_grads = jnp.concatenate(
            [
                return_wide(
                    [
                        rows_contract(
                            all_normed[stream],
                            dquery_rows[stream][:, part * query_half : (part + 1) * query_half],
                        )
                        for stream in range(2)
                    ],
                    query_links[part],
                    None,
                    [(return_events[0],)],
                )
                for part in range(2)
            ],
            axis=1,
        )
        grad_query_w = [query_grads[: query_depth[0]], query_grads[query_depth[0] :]]
        wide_mlp = []
        for i, (gate_w, down_w) in enumerate(((wg_prefix, wd_prefix), (wg_action, wd_action))):
            wide_mlp += [
                jnp.zeros(gate_w.shape, wider),
                jnp.zeros(gate_w.shape, wider),
                jnp.zeros(down_w.shape, wider),
            ]
        for k, packet in packets.items():
            peer = at["wide"] ^ k
            parts = unpack(packet)
            for i in range(6):
                wide_mlp[i] = lax.dynamic_update_slice_in_dim(
                    wide_mlp[i],
                    parts[i].astype(wider),
                    peer * units[i // 3],
                    0 if i % 3 == 2 else 1,
                )

        dnormed_parts = []
        grad_first = []
        for stream in range(2):
            dnormed = cols_contract(keyval_rows[stream], keyval_weight[stream])
            for part in range(2):
                dnormed = dnormed + cols_contract(
                    dquery_rows[stream][:, part * query_half : (part + 1) * query_half],
                    query_weight[stream][part],
                )
            wide_rows = item_rows[stream].astype(wider)
            unit_rows = wide_rows * lax.rsqrt(
                jnp.mean(wide_rows * wide_rows, axis=-1, keepdims=True) + epsilon
            )
            grad_first.append(jnp.sum(dnormed * unit_rows, axis=0))
            dnormed_parts.append(dnormed.astype(low))
        dnormed = streams(
            scatter_rows(jnp.concatenate(dnormed_parts, axis=1), [core, across], [])
        )
        grad_inputs = [
            dmiddle[stream] + norm_back(inputs[stream], first_gain[stream], dnormed[stream])[0]
            for stream in range(2)
        ]
        gain_grads = jnp.concatenate(
            [
                part.reshape(n_all, -1)
                for part in (grad_first[0], grad_second[0], grad_first[1], grad_second[1])
            ],
            axis=1,
        )
        shared_grads = scatter_blocks(
            jnp.concatenate(
                [
                    rows_contract(all_normed[stream], keyval_rows[stream])
                    .astype(low)
                    .reshape(n_all, -1, 2 * head_dim)
                    for stream in range(2)
                ]
                + [pad_gains(gain_grads.astype(low))],
                axis=1,
            ),
            [core, across, side] + far[::-1],
            at,
        )
        grad_keyval_w = [
            shared_grads[: keyval_rows_of[0]],
            shared_grads[keyval_rows_of[0] : gain_start],
        ]
        gain_grads = shared_grads[gain_start]
        small = [
            gain_grads[stop - size : stop]
            for stop, size in zip(gain_stops, gain_sizes, strict=True)
        ]
        mlp_out = streams(
            scatter_all(
                out_most,
                chip_far(out_far, back_events[-1]),
                out_corner[:size],
                out_corner[size:],
                [],
                False,
                [
                    (back_events[-1],),
                    (att_events[0],),
                    (att_events[1],),
                    (return_events[0],),
                    (return_events[1],),
                ],
            )
        )
        outputs = [(middle[stream] + mlp_out[stream]).astype(low) for stream in range(2)]
        weights = [
            (
                grad_query_w[i],
                grad_keyval_w[i][:, :head_dim],
                grad_keyval_w[i][:, head_dim:],
                grad_out_w[i],
                *wide_mlp[3 * i : 3 * i + 3],
                small[2 * i],
                small[2 * i + 1],
            )
            for i in range(2)
        ]
        return (*outputs, *grad_inputs, *weights[0], *weights[1])

    return local


def solution(mesh):
    rows = P(BOTH, None)
    block = P("wide", "narrow")
    turned = P("narrow", "wide")
    vector = P(BOTH)
    weights = (block, rows, rows, turned, block, block, turned, vector, vector)
    return jax.shard_map(
        make_local(mesh.shape["wide"], mesh.shape["narrow"]),
        mesh=mesh,
        in_specs=(
            rows,
            rows,
            rows,
            rows,
            P("wide", None),
            P("wide", None),
            P("wide"),
            P("wide"),
            *weights,
            *weights,
        ),
        out_specs=(rows, rows, rows, rows, *weights, *weights),
        check_vma=False,
    )
```

```python
import functools

import jax
import jax.numpy as jnp
from jax import lax
from jax.experimental import pallas as pl
from jax.experimental.pallas import tpu as pltpu
from jax.sharding import PartitionSpec as P

PREFIX_BLOCKS = 4
BOTH = ("wide", "narrow")

epsilon = 1e-06
scaling = 0.0625
masked_score = -1e30
low = jnp.bfloat16
wider = jnp.float32


def rms_norm(features, weight):
    return (
        features
        * lax.rsqrt(jnp.mean(features * features, axis=-1, keepdims=True) + epsilon)
        * weight
    )


def product(former, latter):
    return jnp.dot(former, latter, preferred_element_type=wider)


def rows_contract(former, latter):
    return lax.dot_general(
        former, latter, (((0,), (0,)), ((), ())), preferred_element_type=wider
    )


def cols_contract(former, latter):
    return lax.dot_general(
        former, latter, (((1,), (1,)), ((), ())), preferred_element_type=wider
    )


def norm_back(features, weight, upstream):
    unused, pullback = jax.vjp(rms_norm, features, weight)
    return pullback(upstream)


def tie(value, *earlier):
    return lax.optimization_barrier((value, *earlier))[0] if earlier else value


def masked_scores(queries, key_rows, allowed):
    scores = jnp.einsum("qhd,kd->hqk", queries, key_rows, preferred_element_type=wider)
    return jnp.where(allowed[None], scores, masked_score)


def copies_kernel(plan, n_in, place_ref, *refs):
    copied = refs[-1]
    copies = []
    for i, (source, source_at, target, target_at) in enumerate(plan):
        source_ref = refs[source].at[source_at(place_ref)]
        target_ref = refs[n_in + target].at[target_at(place_ref)]
        copies.append(pltpu.make_async_copy(source_ref, target_ref, copied.at[i]))
    for copy in copies:
        copy.start()
    for copy in copies:
        copy.wait()


def copy_blocks(plan, places, arrays, shapes, name):
    any_spec = pl.BlockSpec(memory_space=pl.ANY)
    moved = 2 * sum(shape[0] * shape[1] * 2 for shape in shapes)
    return pl.pallas_call(
        functools.partial(copies_kernel, plan, len(arrays)),
        in_specs=[pl.BlockSpec(memory_space=pltpu.SMEM)] + [any_spec] * len(arrays),
        out_specs=[pl.BlockSpec(memory_space=pltpu.VMEM)] * len(shapes),
        scratch_shapes=[pltpu.SemaphoreType.DMA((len(plan),))],
        compiler_params=pltpu.CompilerParams(vmem_limit_bytes=24 << 20),
        out_shape=[jax.ShapeDtypeStruct(shape, low) for shape in shapes],
        cost_estimate=pl.CostEstimate(flops=0, bytes_accessed=moved, transcendentals=0),
        name=name,
    )(places, *arrays)


def block(index, size):
    return pl.ds(pl.multiple_of(index * size, size), size)


def feed_kernel(count, half, n_kept, n_copied, first, *refs):
    token_refs, refs = refs[:count], refs[count:]
    grad_refs, refs = refs[:count], refs[count:]
    weight_refs, refs = refs[:4], refs[4 + n_kept :]
    kept_refs, row_refs = refs[:n_copied], refs[n_copied : n_copied + 4]
    back_ref, out_ref, copied = refs[n_copied + 4 :]
    step = pl.program_id(0)
    tile = token_refs[0].shape[0]
    width = weight_refs[1].shape[1]
    columns_of = (slice(0, width), slice(width, width + weight_refs[3].shape[1]))
    slope = 0.7978845608028654

    def run(token_ref, grad_ref):
        place = block(first + step, tile)
        copies = [
            pltpu.make_async_copy(
                source.at[:, columns_of[i % 2]], kept_refs[i].at[place], copied.at[i]
            )
            for i, source in enumerate((token_ref, token_ref, grad_ref, grad_ref)[:n_copied])
        ]
        for copy in copies:
            copy.start()
        for i, columns in enumerate(columns_of):
            gate_up_ref, down_ref = weight_refs[2 * i : 2 * i + 2]
            hidden_ref, both_ref = row_refs[2 * i : 2 * i + 2]
            units = down_ref.shape[0]
            both = product(token_ref[:, columns], gate_up_ref[...])
            gate, up = both[:, :units], both[:, units:]
            square = gate * gate
            bend = jnp.tanh(slope * gate * (1.0 + 0.044715 * square))
            active = 0.5 * gate * (1.0 + bend)
            hidden = (active * up).astype(low)
            hidden_ref[...] = hidden
            dhidden = cols_contract(grad_ref[:, columns], down_ref[...])
            steep = 0.5 * (1.0 + bend) + 0.5 * gate * (1.0 - bend * bend) * slope * (
                1.0 + 3 * 0.044715 * square
            )
            both_ref[:, :units] = (dhidden * up * steep).astype(low)
            both_ref[:, units:] = (dhidden * active).astype(low)
            back_ref[:, columns] = cols_contract(both_ref[...], gate_up_ref[...]).astype(low)
            out_ref[:, columns] = product(hidden, down_ref[...]).astype(low)
        for copy in copies:
            copy.wait()

    for piece in range(count):
        pl.when(step // half == piece)(
            functools.partial(run, token_refs[piece], grad_refs[piece])
        )


def feed_forward(tokens, grads, weights, kept, size, total, first, n_copied):
    count = len(tokens)
    columns = tokens[0][0].shape[1]
    tile = min(size, 256)
    half = size // tile
    units = [weights[1].shape[0], weights[3].shape[0]]
    widths = [weights[1].shape[1], weights[3].shape[1]]
    first = first * half
    rows = [units[0], 2 * units[0], units[1], 2 * units[1]]
    any_spec = pl.BlockSpec(memory_space=pl.ANY)

    def piece_spec(piece, place):
        return pl.BlockSpec(
            (tile, columns),
            lambda i: (place * half + jnp.clip(i - piece * half, 0, half - 1), 0),
        )

    out = pl.pallas_call(
        functools.partial(feed_kernel, count, half, len(kept), n_copied, first),
        grid=(count * half,),
        in_specs=[piece_spec(i, place) for i, (unused, place) in enumerate(tokens)]
        + [piece_spec(i, place) for i, (unused, place) in enumerate(grads)]
        + [
            pl.BlockSpec(w.shape, lambda i: (0, 0), pipeline_mode=pl.Buffered(1)) for w in weights
        ]
        + [any_spec] * len(kept),
        out_specs=[any_spec] * n_copied
        + [pl.BlockSpec((tile, w), lambda i: (first + i, 0)) for w in rows]
        + [pl.BlockSpec((tile, columns), lambda i: (i, 0))] * 2,
        scratch_shapes=[pltpu.SemaphoreType.DMA((4,))],
        out_shape=[
            jax.ShapeDtypeStruct((total, w), low) for w in (widths * 2)[:n_copied] + rows
        ]
        + [jax.ShapeDtypeStruct((count * size, columns), low)] * 2,
        input_output_aliases={2 * count + 4 + i: i for i in range(len(kept))},
        compiler_params=pltpu.CompilerParams(vmem_limit_bytes=52 << 20),
        cost_estimate=pl.CostEstimate(
            flops=2 * count * size * 6 * (widths[0] * units[0] + widths[1] * units[1]),
            bytes_accessed=12 * count * size * columns,
            transcendentals=0,
        ),
        name="feed_forward",
    )(*(array for array, unused in tokens), *(array for array, unused in grads), *weights, *kept)
    return out[: n_copied + 4], out[n_copied + 4], out[n_copied + 5]


def make_local(n_wide, n_narrow):
    n_all = n_wide * n_narrow
    wide_masks = [1 << bit for bit in range(n_wide.bit_length() - 1)]
    far = [("wide", mask) for mask in wide_masks[:0:-1]]
    side, across, core = ("wide", 1), ("narrow", 2), ("narrow", 1)
    sizes = {"wide": n_wide, "narrow": n_narrow}

    def join(*values):
        return lax.optimization_barrier(values)

    def hop(value, link, *earlier):
        axis, mask = link
        value = tie(value, *earlier)
        return lax.ppermute(value, axis, [(i, i ^ mask) for i in range(sizes[axis])])

    def rank_of(link):
        return link[1] if link[0] == "narrow" else link[1] * n_narrow

    def gather_blocks(block, links, at, events, *earlier):
        held = []
        for i, link in enumerate(links):
            position = sum(other > rank_of(link) for other in held)
            moved = hop(block, link, *(earlier[i] if i < len(earlier) else ()))
            events.append(moved)
            block = jnp.where(
                (at[link[0]] & link[1]) != 0,
                jnp.stack([moved, block], position),
                jnp.stack([block, moved], position),
            )
            held.append(rank_of(link))
        return block.reshape(-1, *block.shape[len(links) :])

    def scatter_blocks(blocks, links, at):
        held = sorted((rank_of(link) for link in links), reverse=True)
        blocks = blocks.reshape(*(2 for unused in links), *blocks.shape[1:])
        for stage, link in enumerate(links):
            position = held.index(rank_of(link))
            bit = jnp.minimum(at[link[0]] & link[1], 1)
            mine = lax.dynamic_index_in_dim(blocks, bit, position, keepdims=False)
            theirs = lax.dynamic_index_in_dim(blocks, 1 - bit, position, keepdims=False)
            blocks = mine.astype(wider) + hop(theirs, link).astype(wider)
            if stage + 1 < len(links):
                blocks = blocks.astype(low)
            held.remove(rank_of(link))
        return blocks

    def gather_rows(rows, links, events=None, *earlier):
        for link in links:
            moved = hop(rows, link, *earlier)
            earlier = ()
            if events is not None:
                events.append(moved)
            rows = jnp.concatenate([rows, moved], axis=0)
        return rows

    def scatter_rows(rows, links, events=None):
        for stage, link in enumerate(links):
            half = rows.shape[0] // 2
            moved = hop(rows[half:], link)
            if events is not None:
                events.append(moved)
            rows = rows[:half].astype(wider) + moved.astype(wider)
            if stage + 1 < len(links):
                rows = rows.astype(low)
        return rows

    def gather_all(rows, events, even, *earlier):
        own = gather_rows(rows, far, events, *earlier)
        from_x, from_y = hop(own, across), hop(own, side)
        half = own.shape[0] // 2
        if even:
            corner = jnp.concatenate(
                [hop(from_y[:half], across), hop(from_x[half:], side)], axis=0
            )
        else:
            corner = hop(from_y, across)
        return own, from_x, from_y, corner

    def scatter_all(most, other_most, corner, other_corner, events, even, *earlier):
        corner = corner.astype(wider) + hop(other_corner, core, *earlier).astype(wider)
        corner = corner.astype(low)
        size = corner.shape[0]
        half = size // 2 if even else size
        for_y = hop(corner[:half], across)
        events.append(for_y)
        if n_all * 64 <= 4096:
            most = most.astype(wider) + hop(other_most, core, *earlier).astype(wider)
            own, sum_x, sum_y = (most[i * size : (i + 1) * size] for i in range(3))
        else:
            parts = [slice(i * size, (i + 1) * size) for i in range(3)]
            own, sum_x, sum_y = (
                most[rows].astype(wider) + hop(other_most[rows], core, *earlier).astype(wider)
                for rows in parts
            )
        if even:
            for_x = hop(corner[half:], side)
            sum_x = jnp.concatenate([sum_x[:half], sum_x[half:] + for_x.astype(wider)], axis=0)
            sum_y = jnp.concatenate([sum_y[:half] + for_y.astype(wider), sum_y[half:]], axis=0)
        else:
            sum_y = sum_y + for_y.astype(wider)
        moved_x, moved_y = hop(sum_x.astype(low), across), hop(sum_y.astype(low), side)
        events.append(moved_y)
        total = own + moved_x.astype(wider) + moved_y.astype(wider)
        return scatter_rows(total.astype(low), far[::-1], events)

    def local(
        x_prefix,
        x_action,
        cot_prefix,
        cot_action,
        prefix_block,
        action_block,
        valid_len,
        mix_weight,
        wq_prefix,
        wk_prefix,
        wv_prefix,
        wo_prefix,
        wg_prefix,
        wu_prefix,
        wd_prefix,
        norm1_prefix,
        norm2_prefix,
        wq_action,
        wk_action,
        wv_action,
        wo_action,
        wg_action,
        wu_action,
        wd_action,
        norm1_action,
        norm2_action,
    ):
        at = {"wide": lax.axis_index("wide"), "narrow": lax.axis_index("narrow")}
        head_dim = wk_prefix.shape[1]
        own = x_prefix.shape[0]
        width = x_prefix.shape[1]

        def streams(packed):
            return [packed[:, :width], packed[:, width:]]

        depth = [wg_prefix.shape[0], wg_action.shape[0]]
        units = [wg_prefix.shape[1] // n_wide, wg_action.shape[1] // n_wide]

        def fold(rows, lead):
            return jnp.concatenate(
                [rows[i * lead : (i + 1) * lead] for i in range(rows.shape[0] // lead)], axis=1
            )

        def unfold(rows, columns):
            return jnp.concatenate(
                [
                    rows[:, i * columns : (i + 1) * columns]
                    for i in range(rows.shape[1] // columns)
                ],
                axis=0,
            )

        def pack(parts):
            gate_p, up_p, down_p, gate_a, up_a, down_a = parts
            action = jnp.concatenate([gate_a, up_a, fold(down_a, depth[1])], axis=1)
            action = jnp.pad(action, [(0, 0), (0, units[0] - action.shape[1])])
            return jnp.concatenate([gate_p, up_p, fold(down_p, depth[0]), action], axis=0)

        def unpack(packet):
            d, f = depth[0], units[1]
            action = packet[3 * d :]
            return (
                packet[:d],
                packet[d : 2 * d],
                unfold(packet[2 * d : 3 * d], d),
                action[:, :f],
                action[:, f : 2 * f],
                unfold(action[:, 2 * f : 3 * f], depth[1]),
            )

        distances = list(range(1, n_wide))

        aligned = units[1] % 128 == 0 and depth[1] % 16 == 0 and units[1] == depth[1]
        folds = units[0] // depth[0]
        packet_shape = (3 * depth[0] + depth[1], units[0])
        peers = at["wide"] ^ jnp.arange(n_wide, dtype=jnp.int32)

        def packet_plan(outward, blocks_of):
            plan = []
            for k in range(n_wide):
                for array, array_at, packet_at in blocks_of(k):
                    if outward:
                        plan.append((array, array_at, k, lambda ref, at=packet_at: at))
                    else:
                        plan.append((k, lambda ref, at=packet_at: at, array, array_at))
            return plan

        def span(start, size):
            return slice(start, start + size)

        def packet_places(k, gate_at, up_at, down_at, arrays):
            for i, (d, f) in enumerate(zip(depth, units, strict=True)):
                gate, up, down = arrays[3 * i : 3 * i + 3]
                top = 3 * depth[0] if i else 0
                second = (span(top, d), span(f, f)) if i else (span(d, d), span(0, f))
                yield gate, functools.partial(gate_at, k, d, f), (span(top, d), span(0, f))
                yield up, functools.partial(up_at, k, d, f), second
                for part in range(f // d):
                    place = (span(top, d), span(2 * f, d)) if i else (span(2 * d, d), span(part * d, d))
                    yield down, functools.partial(down_at, k, d, f, part), place

        def weight_packet(k):
            peer = at["wide"] ^ k
            f, g = units
            return pack(
                (
                    lax.dynamic_slice_in_dim(wg_prefix, peer * f, f, 1),
                    lax.dynamic_slice_in_dim(wu_prefix, peer * f, f, 1),
                    lax.dynamic_slice_in_dim(wd_prefix, peer * f, f, 0),
                    lax.dynamic_slice_in_dim(wg_action, peer * g, g, 1),
                    lax.dynamic_slice_in_dim(wu_action, peer * g, g, 1),
                    lax.dynamic_slice_in_dim(wd_action, peer * g, g, 0),
                )
            )

        if aligned:
            packets = copy_blocks(
                packet_plan(
                    True,
                    lambda k: packet_places(
                        k,
                        lambda k, d, f, ref: (slice(None), block(ref[k], f)),
                        lambda k, d, f, ref: (slice(None), block(ref[k], f)),
                        lambda k, d, f, part, ref: (
                            pl.ds(pl.multiple_of(ref[k] * f, f) + part * d, d),
                            slice(None),
                        ),
                        range(6),
                    ),
                ),
                peers,
                [wg_prefix, wu_prefix, wd_prefix, wg_action, wu_action, wd_action],
                [packet_shape] * n_wide,
                "pack_weights",
            )
            packets = dict(enumerate(packets))
            weight_packet = packets.get
        else:
            packets = {0: weight_packet(0)}

        narrow_links = [across, core]
        x_packed = jnp.concatenate([x_prefix, x_action], axis=1)
        item_packed = gather_rows(x_packed, narrow_links)
        item_rows = streams(item_packed)

        gain_parts = [norm1_prefix, norm2_prefix, norm1_action, norm2_action]
        gain_sizes = [part.shape[0] for part in gain_parts]
        gain_stops = [sum(gain_sizes[: i + 1]) for i in range(4)]
        keyval_rows_of = [wk_prefix.shape[0], wk_action.shape[0]]
        gain_start = sum(keyval_rows_of)
        gain_rows = 16

        def pad_gains(row):
            return jnp.pad(
                row[..., None, :],
                [(0, 0)] * (row.ndim - 1) + [(0, gain_rows - 1), (0, 2 * head_dim - row.shape[-1])],
            )

        shared_events, query_events, out_events = [], [], []
        shared = gather_blocks(
            jnp.concatenate(
                [
                    jnp.concatenate([wk_prefix, wv_prefix], axis=1),
                    jnp.concatenate([wk_action, wv_action], axis=1),
                    pad_gains(jnp.concatenate(gain_parts)),
                ],
                axis=0,
            ),
            far + [side, across, core],
            at,
            shared_events,
        )
        gains_all = shared[:, gain_start, :].astype(wider)
        gains = [
            gains_all[:, stop - size : stop].reshape(-1)
            for stop, size in zip(gain_stops, gain_sizes, strict=True)
        ]
        first_gain = [gains[0], gains[2]]
        second_gain = [gains[1], gains[3]]
        keyval_weight = [
            shared[:, : keyval_rows_of[0]].reshape(-1, 2 * head_dim),
            shared[:, keyval_rows_of[0] : gain_start].reshape(-1, 2 * head_dim),
        ]
        query_depth = [wq_prefix.shape[0], wq_action.shape[0]]
        query_half = wq_prefix.shape[1] // 2
        query_packed = jnp.concatenate([wq_prefix, wq_action], axis=0)
        wide_links = far + [side]
        query_blocks = [
            gather_blocks(query_packed[:, :query_half], wide_links, at, []),
            gather_blocks(
                query_packed[:, query_half:],
                [side] + far,
                at,
                query_events,
                (),
                (packets[max(packets)],),
            ),
        ]
        query_weight = [
            [blocks[:, : query_depth[0]].reshape(-1, query_half) for blocks in query_blocks],
            [blocks[:, query_depth[0] :].reshape(-1, query_half) for blocks in query_blocks],
        ]
        out_blocks = gather_blocks(
            jnp.concatenate([wo_prefix.T, wo_action.T], axis=0),
            wide_links,
            at,
            out_events,
            (query_events[1],),
        )
        out_weight = [
            out_blocks[:, : query_depth[0]].reshape(-1, wo_prefix.shape[0]),
            out_blocks[:, query_depth[0] :].reshape(-1, wo_action.shape[0]),
        ]
        item_weight = mix_weight[0]
        dout = jnp.concatenate([cot_prefix, cot_action], axis=1).astype(wider) * item_weight
        grad_events = []
        grad_near = gather_all(dout.astype(low), grad_events, False, shared_events[-3])
        copying = n_all * own <= 4096
        if copying:
            grad_near = jnp.concatenate(grad_near, axis=0)
            grad_far = hop(grad_near, core)
            grad_near, grad_far = ([(rows, i) for i in range(4)] for rows in (grad_near, grad_far))
        else:
            grad_far = [(hop(rows, core), 0) for rows in grad_near]
            grad_near = [(rows, 0) for rows in grad_near]
        def send_packets(few, packet_of, *earlier):
            for k in few:
                packets[k] = hop(packet_of(k), ("wide", k), *earlier)

        def share(first, last):
            return [k for k in distances if first * n_wide <= 8 * k < last * n_wide]

        send_packets(share(4, 5), weight_packet, query_events[0])
        send_packets(share(5, 6), weight_packet, shared_events[-2])
        send_packets(share(0, 2), weight_packet, shared_events[-2])

        all_normed = [
            rms_norm(item_rows[stream].astype(wider), first_gain[stream]).astype(low)
            for stream in range(2)
        ]
        prefix_len = item_packed.shape[0]
        total_rows = 2 * prefix_len
        joined = jnp.concatenate(
            [
                product(all_normed[stream], keyval_weight[stream]).astype(low)
                for stream in range(2)
            ],
            axis=0,
        )
        key_rows = joined[:, :head_dim]
        values = joined[:, head_dim:]
        queries = jnp.concatenate(
            [
                jnp.concatenate(
                    [
                        (product(all_normed[stream], part) * scaling).astype(low)
                        for part in query_weight[stream]
                    ],
                    axis=1,
                )
                for stream in range(2)
            ],
            axis=0,
        ).reshape(total_rows, -1, head_dim)
        offsets = [0]
        for unused, mask in narrow_links:
            offsets = offsets + [offset ^ mask for offset in offsets]
        owners = at["narrow"] ^ jnp.array(offsets, jnp.int32)

        def reorder(ids):
            return jnp.take(ids.reshape(n_narrow, -1), owners, axis=0).reshape(-1)

        blocks = jnp.concatenate(
            [reorder(prefix_block[0]), reorder(action_block[0]) + PREFIX_BLOCKS]
        )
        positions = (owners[:, None] * own + jnp.arange(own, dtype=jnp.int32)[None]).reshape(-1)
        usable = jnp.concatenate(
            [
                positions < valid_len[0],
                jnp.ones((total_rows - prefix_len,), dtype=jnp.bool_),
            ]
        )
        allowed = (blocks[None, :] <= blocks[:, None]) & usable[None, :]
        scores = masked_scores(queries, key_rows, allowed)
        highest = jnp.max(scores, axis=-1, keepdims=True)
        exponent = jnp.exp(scores - highest)
        denominator = jnp.sum(exponent, axis=-1, keepdims=True)
        log_total = highest + jnp.log(denominator)
        attention = (exponent / denominator).astype(low)
        mixed_all = jnp.einsum("hqk,kd->qhd", attention, values, preferred_element_type=wider)
        mixed_all = mixed_all.astype(low).reshape(total_rows, -1)
        mixed_rows = [mixed_all[:prefix_len], mixed_all[prefix_len:]]
        attended_all = (
            jnp.concatenate(
                [
                    cols_contract(mixed_rows[stream], out_weight[stream]).astype(low)
                    for stream in range(2)
                ],
                axis=1,
            )
        )
        attended_events = []
        attended_all = tie(attended_all, packets[n_wide // 2], *grad_events)
        attended = scatter_rows(attended_all, [core, across], attended_events)
        send_packets(share(7, 8), weight_packet, attended_events[1])
        send_packets(share(3, 4), weight_packet, attended_events[1])
        inputs = [x_prefix.astype(wider), x_action.astype(wider)]
        middle = [
            rows + part for rows, part in zip(inputs, streams(attended), strict=True)
        ]
        normed2 = jnp.concatenate(
            [rms_norm(middle[stream], second_gain[stream]).astype(low) for stream in range(2)],
            axis=1,
        )
        token_events = []
        normed2 = tie(normed2, *(packets[k] for k in share(5, 6) + share(0, 2)))
        near = gather_all(normed2, token_events, True)
        if copying:
            other_most = hop(jnp.concatenate(near[:3], axis=0), core)
            token_far = [(other_most, i) for i in range(3)] + [(hop(near[3], core), 0)]
        else:
            token_far = [(hop(rows, core), 0) for rows in near]
        send_packets(share(6, 7), weight_packet, token_events[-1])
        send_packets(share(2, 3), weight_packet, token_events[-1])
        if aligned:
            feed_weights = copy_blocks(
                packet_plan(
                    False,
                    lambda k: packet_places(
                        k,
                        lambda k, d, f, ref: (block(ref[k], d), span(0, f)),
                        lambda k, d, f, ref: (block(ref[k], d), span(f, f)),
                        lambda k, d, f, part, ref: (span(part * d, d), block(ref[k], d)),
                        (0, 0, 1, 2, 2, 3),
                    ),
                ),
                peers,
                [packets[k] for k in range(n_wide)],
                [
                    (depth[0] * n_wide, 2 * units[0]),
                    (units[0], depth[0] * n_wide),
                    (depth[1] * n_wide, 2 * units[1]),
                    (units[1], depth[1] * n_wide),
                ],
                "unpack_weights",
            )
        else:
            gate_up_weight = [jnp.zeros((depth[i] * n_wide, 2 * units[i]), low) for i in range(2)]
            down_weight = [jnp.zeros((units[i], depth[i] * n_wide), low) for i in range(2)]
            for k, packet in packets.items():
                peer = at["wide"] ^ k
                parts = unpack(packet)
                for i in range(2):
                    gate_up_weight[i] = lax.dynamic_update_slice_in_dim(
                        gate_up_weight[i],
                        jnp.concatenate(parts[3 * i : 3 * i + 2], axis=1),
                        peer * depth[i],
                        0,
                    )
                    down_weight[i] = lax.dynamic_update_slice_in_dim(
                        down_weight[i], parts[3 * i + 2], peer * depth[i], 1
                    )
            feed_weights = [gate_up_weight[0], down_weight[0], gate_up_weight[1], down_weight[1]]

        size = near[0].shape[0]
        feed = functools.partial(
            feed_forward,
            weights=feed_weights,
            size=size,
            total=n_all * own,
            n_copied=4 if copying else 0,
        )
        token_pieces = [(rows, 0) for rows in near] + [token_far[3], *token_far[:3]]
        grad_pieces = [*grad_near, grad_far[3], *grad_far[:3]]
        kept, back_most, out_most = feed(token_pieces[:3], grad_pieces[:3], kept=[], first=0)
        kept, back_corner, out_corner = feed(
            token_pieces[3:5], grad_pieces[3:5], kept=kept, first=3
        )
        kept, back_far, out_far = feed(token_pieces[5:], grad_pieces[5:], kept=kept, first=5)
        hidden_rows, both_rows = kept[-4::2], kept[-3::2]
        if not copying:
            gate_up_grad = [0.0, 0.0]
            down_grad = [0.0, 0.0]
            for i, ((token, token_at), (grad, grad_at)) in enumerate(
                zip(token_pieces, grad_pieces, strict=True)
            ):
                rows = slice(i * size, (i + 1) * size)
                token = streams(token[token_at * size : (token_at + 1) * size])
                grad = streams(grad[grad_at * size : (grad_at + 1) * size])
                for j in range(2):
                    gate_up_grad[j] = gate_up_grad[j] + rows_contract(token[j], both_rows[j][rows])
                    down_grad[j] = down_grad[j] + rows_contract(hidden_rows[j][rows], grad[j])
            gate_up_grad = [grad.astype(low) for grad in gate_up_grad]
            down_grad = [grad.astype(low) for grad in down_grad]
            back_corner, back_far, out_corner, out_far, *held = join(
                back_corner, back_far, out_corner, out_far, *gate_up_grad, *down_grad
            )
            gate_up_grad, down_grad = held[:2], held[2:]
        back_events = []
        dnormed2_packed = scatter_all(
            back_most, back_far, back_corner[:size], back_corner[size:], back_events, True
        )
        dnormed2 = streams(dnormed2_packed)
        mlp_out = streams(
            scatter_all(
                out_most, out_far, out_corner[:size], out_corner[size:], [], False, back_events[-1]
            )
        )
        if copying:
            gate_up_grad = [rows_contract(kept[i], both_rows[i]) for i in range(2)]
            down_grad = [rows_contract(hidden_rows[i], kept[2 + i]) for i in range(2)]
            gate_up_grad = [grad.astype(low) for grad in gate_up_grad]
            down_grad = [grad.astype(low) for grad in down_grad]

        def gradient_packet(k):
            peer = at["wide"] ^ k
            parts = []
            for i in range(2):
                both = lax.dynamic_slice_in_dim(gate_up_grad[i], peer * depth[i], depth[i], 0)
                down = lax.dynamic_slice_in_dim(down_grad[i], peer * depth[i], depth[i], 1)
                parts += [both[:, : units[i]], both[:, units[i] :], down]
            return pack(parts)

        if aligned:
            packets = copy_blocks(
                packet_plan(
                    True,
                    lambda k: packet_places(
                        k,
                        lambda k, d, f, ref: (block(ref[k], d), span(0, f)),
                        lambda k, d, f, ref: (block(ref[k], d), span(f, f)),
                        lambda k, d, f, part, ref: (span(part * d, d), block(ref[k], d)),
                        (0, 0, 1, 2, 2, 3),
                    ),
                ),
                peers,
                [gate_up_grad[0], down_grad[0], gate_up_grad[1], down_grad[1]],
                [packet_shape] * n_wide,
                "pack_gradients",
            )
            packets = dict(enumerate(packets))
            gradient_packet = packets.get
        else:
            packets = {0: gradient_packet(0)}
        send_packets(share(4, 5), gradient_packet)
        send_packets(share(2, 3), gradient_packet)
        send_packets(share(6, 7), gradient_packet, back_events[1])
        send_packets(share(0, 2), gradient_packet, back_events[-1])
        send_packets(share(5, 6), gradient_packet, back_events[-1])
        outputs = [(middle[stream] + mlp_out[stream]).astype(low) for stream in range(2)]
        dmiddle = []
        grad_second = []
        for stream, dout_part in enumerate(streams(dout)):
            from_norm, gain_part = norm_back(middle[stream], second_gain[stream], dnormed2[stream])
            dmiddle.append(dout_part + from_norm)
            grad_second.append(gain_part)
        att_events = []
        grad_att = streams(
            gather_rows(
                tie(
                    jnp.concatenate([part.astype(low) for part in dmiddle], axis=1),
                    *(packets[k] for k in share(4, 5) + share(2, 3)),
                ),
                narrow_links,
                att_events,
            )
        )
        send_packets(share(7, 8), gradient_packet, att_events[0])
        send_packets(share(3, 4), gradient_packet, att_events[0])

        def return_wide(parts, links):
            blocks = jnp.concatenate(
                [part.astype(low).reshape(n_wide, -1, part.shape[1]) for part in parts], axis=1
            )
            return scatter_blocks(blocks, links, at)

        out_grads = return_wide(
            [rows_contract(grad_att[stream], mixed_rows[stream]) for stream in range(2)],
            wide_links[::-1],
        )
        grad_out_w = [out_grads[: query_depth[0]].T, out_grads[query_depth[0] :].T]
        dmixed = jnp.concatenate(
            [product(grad_att[stream], out_weight[stream]) for stream in range(2)],
            axis=0,
        )
        dmixed = dmixed.astype(low).reshape(total_rows, -1, head_dim)
        recomputed = jnp.exp(masked_scores(queries, key_rows, allowed) - log_total)
        dprobs = jnp.einsum("qhd,kd->hqk", dmixed, values, preferred_element_type=wider)
        row_inner = jnp.sum(recomputed * dprobs, axis=-1, keepdims=True)
        dscores = (recomputed * (dprobs - row_inner)).astype(low)
        dquery = jnp.einsum("hqk,kd->qhd", dscores, key_rows, preferred_element_type=wider)
        dquery = (dquery.astype(low) * scaling).reshape(total_rows, -1)
        grad_key = jnp.einsum("hqk,qhd->kd", dscores, queries, preferred_element_type=wider)
        dvalue = jnp.einsum(
            "hqk,qhd->kd", recomputed.astype(low), dmixed, preferred_element_type=wider
        )
        grad_keyval = jnp.concatenate([grad_key, dvalue], axis=1).astype(low)
        dquery_rows = [dquery[:prefix_len], dquery[prefix_len:]]
        keyval_rows = [grad_keyval[:prefix_len], grad_keyval[prefix_len:]]
        query_links = [[side] + far[::-1], far[::-1] + [side]]
        query_grads = jnp.concatenate(
            [
                return_wide(
                    [
                        rows_contract(
                            all_normed[stream],
                            dquery_rows[stream][:, part * query_half : (part + 1) * query_half],
                        )
                        for stream in range(2)
                    ],
                    query_links[part],
                )
                for part in range(2)
            ],
            axis=1,
        )
        grad_query_w = [query_grads[: query_depth[0]], query_grads[query_depth[0] :]]
        wide_mlp = []
        for i, (gate_w, down_w) in enumerate(((wg_prefix, wd_prefix), (wg_action, wd_action))):
            wide_mlp += [
                jnp.zeros(gate_w.shape, wider),
                jnp.zeros(gate_w.shape, wider),
                jnp.zeros(down_w.shape, wider),
            ]
        for k, packet in packets.items():
            peer = at["wide"] ^ k
            parts = unpack(packet)
            for i in range(6):
                wide_mlp[i] = lax.dynamic_update_slice_in_dim(
                    wide_mlp[i],
                    parts[i].astype(wider),
                    peer * units[i // 3],
                    0 if i % 3 == 2 else 1,
                )

        dnormed_parts = []
        grad_first = []
        for stream in range(2):
            dnormed = cols_contract(keyval_rows[stream], keyval_weight[stream])
            for part in range(2):
                dnormed = dnormed + cols_contract(
                    dquery_rows[stream][:, part * query_half : (part + 1) * query_half],
                    query_weight[stream][part],
                )
            wide_rows = item_rows[stream].astype(wider)
            unit_rows = wide_rows * lax.rsqrt(
                jnp.mean(wide_rows * wide_rows, axis=-1, keepdims=True) + epsilon
            )
            grad_first.append(jnp.sum(dnormed * unit_rows, axis=0))
            dnormed_parts.append(dnormed.astype(low))
        dnormed = streams(
            scatter_rows(jnp.concatenate(dnormed_parts, axis=1), [core, across])
        )
        grad_inputs = [
            dmiddle[stream] + norm_back(inputs[stream], first_gain[stream], dnormed[stream])[0]
            for stream in range(2)
        ]
        gain_grads = jnp.concatenate(
            [
                part.reshape(n_all, -1)
                for part in (grad_first[0], grad_second[0], grad_first[1], grad_second[1])
            ],
            axis=1,
        )
        shared_grads = scatter_blocks(
            jnp.concatenate(
                [
                    rows_contract(all_normed[stream], keyval_rows[stream])
                    .astype(low)
                    .reshape(n_all, -1, 2 * head_dim)
                    for stream in range(2)
                ]
                + [pad_gains(gain_grads.astype(low))],
                axis=1,
            ),
            [core, across, side] + far[::-1],
            at,
        )
        grad_keyval_w = [
            shared_grads[: keyval_rows_of[0]],
            shared_grads[keyval_rows_of[0] : gain_start],
        ]
        gain_grads = shared_grads[gain_start]
        small = [
            gain_grads[stop - size : stop]
            for stop, size in zip(gain_stops, gain_sizes, strict=True)
        ]
        weights = [
            (
                grad_query_w[i],
                grad_keyval_w[i][:, :head_dim],
                grad_keyval_w[i][:, head_dim:],
                grad_out_w[i],
                *wide_mlp[3 * i : 3 * i + 3],
                small[2 * i],
                small[2 * i + 1],
            )
            for i in range(2)
        ]
        return (*outputs, *grad_inputs, *weights[0], *weights[1])

    return local


def solution(mesh):
    rows = P(BOTH, None)
    block = P("wide", "narrow")
    turned = P("narrow", "wide")
    vector = P(BOTH)
    weights = (block, rows, rows, turned, block, block, turned, vector, vector)
    return jax.shard_map(
        make_local(mesh.shape["wide"], mesh.shape["narrow"]),
        mesh=mesh,
        in_specs=(
            rows,
            rows,
            rows,
            rows,
            P("wide", None),
            P("wide", None),
            P("wide"),
            P("wide"),
            *weights,
            *weights,
        ),
        out_specs=(rows, rows, rows, rows, *weights, *weights),
        check_vma=False,
    )
```

```python
import functools

import jax
import jax.numpy as jnp
from jax import lax
from jax.experimental import pallas as pl
from jax.experimental.pallas import tpu as pltpu
from jax.sharding import PartitionSpec as P

PREFIX_BLOCKS = 4
BOTH = ("wide", "narrow")

epsilon = 1e-06
scaling = 0.0625
masked_score = -1e30
low = jnp.bfloat16
wider = jnp.float32


def rms_norm(features, weight):
    return (
        features
        * lax.rsqrt(jnp.mean(features * features, axis=-1, keepdims=True) + epsilon)
        * weight
    )


def product(former, latter):
    return jnp.dot(former, latter, preferred_element_type=wider)


def rows_contract(former, latter):
    return lax.dot_general(
        former, latter, (((0,), (0,)), ((), ())), preferred_element_type=wider
    )


def cols_contract(former, latter):
    return lax.dot_general(
        former, latter, (((1,), (1,)), ((), ())), preferred_element_type=wider
    )


def norm_back(features, weight, upstream):
    unused, pullback = jax.vjp(rms_norm, features, weight)
    return pullback(upstream)


def tie(value, *earlier):
    return lax.optimization_barrier((value, *earlier))[0] if earlier else value


def masked_scores(queries, key_rows, allowed):
    scores = jnp.einsum("qhd,kd->hqk", queries, key_rows, preferred_element_type=wider)
    return jnp.where(allowed[None], scores, masked_score)


def copies_kernel(plan, n_in, place_ref, *refs):
    copied = refs[-1]
    copies = []
    for i, (source, source_at, target, target_at) in enumerate(plan):
        source_ref = refs[source].at[source_at(place_ref)]
        target_ref = refs[n_in + target].at[target_at(place_ref)]
        copies.append(pltpu.make_async_copy(source_ref, target_ref, copied.at[i]))
    for copy in copies:
        copy.start()
    for copy in copies:
        copy.wait()


def copy_blocks(plan, places, arrays, shapes, name):
    any_spec = pl.BlockSpec(memory_space=pl.ANY)
    moved = 2 * sum(shape[0] * shape[1] * 2 for shape in shapes)
    return pl.pallas_call(
        functools.partial(copies_kernel, plan, len(arrays)),
        in_specs=[pl.BlockSpec(memory_space=pltpu.SMEM)] + [any_spec] * len(arrays),
        out_specs=[pl.BlockSpec(memory_space=pltpu.VMEM)] * len(shapes),
        scratch_shapes=[pltpu.SemaphoreType.DMA((len(plan),))],
        compiler_params=pltpu.CompilerParams(vmem_limit_bytes=24 << 20),
        out_shape=[jax.ShapeDtypeStruct(shape, low) for shape in shapes],
        cost_estimate=pl.CostEstimate(flops=0, bytes_accessed=moved, transcendentals=0),
        name=name,
    )(places, *arrays)


def block(index, size):
    return pl.ds(pl.multiple_of(index * size, size), size)


def feed_kernel(count, half, n_kept, n_copied, first, *refs):
    token_refs, refs = refs[:count], refs[count:]
    grad_refs, refs = refs[:count], refs[count:]
    weight_refs, refs = refs[:4], refs[4 + n_kept :]
    kept_refs, row_refs = refs[:n_copied], refs[n_copied : n_copied + 4]
    back_ref, out_ref, copied = refs[n_copied + 4 :]
    step = pl.program_id(0)
    tile = token_refs[0].shape[0]
    width = weight_refs[1].shape[1]
    columns_of = (slice(0, width), slice(width, width + weight_refs[3].shape[1]))
    slope = 0.7978845608028654

    def run(token_ref, grad_ref):
        place = block(first + step, tile)
        copies = [
            pltpu.make_async_copy(
                source.at[:, columns_of[i % 2]], kept_refs[i].at[place], copied.at[i]
            )
            for i, source in enumerate((token_ref, token_ref, grad_ref, grad_ref)[:n_copied])
        ]
        for copy in copies:
            copy.start()
        for i, columns in enumerate(columns_of):
            gate_up_ref, down_ref = weight_refs[2 * i : 2 * i + 2]
            hidden_ref, both_ref = row_refs[2 * i : 2 * i + 2]
            units = down_ref.shape[0]
            both = product(token_ref[:, columns], gate_up_ref[...])
            gate, up = both[:, :units], both[:, units:]
            square = gate * gate
            bend = jnp.tanh(slope * gate * (1.0 + 0.044715 * square))
            active = 0.5 * gate * (1.0 + bend)
            hidden = (active * up).astype(low)
            hidden_ref[...] = hidden
            dhidden = cols_contract(grad_ref[:, columns], down_ref[...])
            steep = 0.5 * (1.0 + bend) + 0.5 * gate * (1.0 - bend * bend) * slope * (
                1.0 + 3 * 0.044715 * square
            )
            both_ref[:, :units] = (dhidden * up * steep).astype(low)
            both_ref[:, units:] = (dhidden * active).astype(low)
            back_ref[:, columns] = cols_contract(both_ref[...], gate_up_ref[...]).astype(low)
            out_ref[:, columns] = product(hidden, down_ref[...]).astype(low)
        for copy in copies:
            copy.wait()

    for piece in range(count):
        pl.when(step // half == piece)(
            functools.partial(run, token_refs[piece], grad_refs[piece])
        )


def feed_forward(tokens, grads, weights, kept, size, total, first, n_copied):
    count = len(tokens)
    columns = tokens[0][0].shape[1]
    tile = min(size, 256)
    half = size // tile
    units = [weights[1].shape[0], weights[3].shape[0]]
    widths = [weights[1].shape[1], weights[3].shape[1]]
    first = first * half
    rows = [units[0], 2 * units[0], units[1], 2 * units[1]]
    any_spec = pl.BlockSpec(memory_space=pl.ANY)

    def piece_spec(piece, place):
        return pl.BlockSpec(
            (tile, columns),
            lambda i: (place * half + jnp.clip(i - piece * half, 0, half - 1), 0),
        )

    out = pl.pallas_call(
        functools.partial(feed_kernel, count, half, len(kept), n_copied, first),
        grid=(count * half,),
        in_specs=[piece_spec(i, place) for i, (unused, place) in enumerate(tokens)]
        + [piece_spec(i, place) for i, (unused, place) in enumerate(grads)]
        + [
            pl.BlockSpec(w.shape, lambda i: (0, 0), pipeline_mode=pl.Buffered(1)) for w in weights
        ]
        + [any_spec] * len(kept),
        out_specs=[any_spec] * n_copied
        + [pl.BlockSpec((tile, w), lambda i: (first + i, 0)) for w in rows]
        + [pl.BlockSpec((tile, columns), lambda i: (i, 0))] * 2,
        scratch_shapes=[pltpu.SemaphoreType.DMA((4,))],
        out_shape=[
            jax.ShapeDtypeStruct((total, w), low) for w in (widths * 2)[:n_copied] + rows
        ]
        + [jax.ShapeDtypeStruct((count * size, columns), low)] * 2,
        input_output_aliases={2 * count + 4 + i: i for i in range(len(kept))},
        compiler_params=pltpu.CompilerParams(vmem_limit_bytes=52 << 20),
        cost_estimate=pl.CostEstimate(
            flops=2 * count * size * 6 * (widths[0] * units[0] + widths[1] * units[1]),
            bytes_accessed=12 * count * size * columns,
            transcendentals=0,
        ),
        name="feed_forward",
    )(*(array for array, unused in tokens), *(array for array, unused in grads), *weights, *kept)
    return out[: n_copied + 4], out[n_copied + 4], out[n_copied + 5]


def make_local(n_wide, n_narrow):
    n_all = n_wide * n_narrow
    wide_masks = [1 << bit for bit in range(n_wide.bit_length() - 1)]
    far = [("wide", mask) for mask in wide_masks[:0:-1]]
    side, across, core = ("wide", 1), ("narrow", 2), ("narrow", 1)
    sizes = {"wide": n_wide, "narrow": n_narrow}

    def join(*values):
        return lax.optimization_barrier(values)

    def hop(value, link, *earlier):
        axis, mask = link
        value = tie(value, *earlier)
        return lax.ppermute(value, axis, [(i, i ^ mask) for i in range(sizes[axis])])

    def rank_of(link):
        return link[1] if link[0] == "narrow" else link[1] * n_narrow

    def gather_blocks(block, links, at, events, *earlier):
        held = []
        for i, link in enumerate(links):
            position = sum(other > rank_of(link) for other in held)
            moved = hop(block, link, *(earlier[i] if i < len(earlier) else ()))
            events.append(moved)
            block = jnp.where(
                (at[link[0]] & link[1]) != 0,
                jnp.stack([moved, block], position),
                jnp.stack([block, moved], position),
            )
            held.append(rank_of(link))
        return block.reshape(-1, *block.shape[len(links) :])

    def scatter_blocks(blocks, links, at):
        held = sorted((rank_of(link) for link in links), reverse=True)
        blocks = blocks.reshape(*(2 for unused in links), *blocks.shape[1:])
        for stage, link in enumerate(links):
            position = held.index(rank_of(link))
            bit = jnp.minimum(at[link[0]] & link[1], 1)
            mine = lax.dynamic_index_in_dim(blocks, bit, position, keepdims=False)
            theirs = lax.dynamic_index_in_dim(blocks, 1 - bit, position, keepdims=False)
            blocks = mine.astype(wider) + hop(theirs, link).astype(wider)
            if stage + 1 < len(links):
                blocks = blocks.astype(low)
            held.remove(rank_of(link))
        return blocks

    def gather_rows(rows, links, events=None, *earlier):
        for link in links:
            moved = hop(rows, link, *earlier)
            earlier = ()
            if events is not None:
                events.append(moved)
            rows = jnp.concatenate([rows, moved], axis=0)
        return rows

    def scatter_rows(rows, links, events=None):
        for stage, link in enumerate(links):
            half = rows.shape[0] // 2
            moved = hop(rows[half:], link)
            if events is not None:
                events.append(moved)
            rows = rows[:half].astype(wider) + moved.astype(wider)
            if stage + 1 < len(links):
                rows = rows.astype(low)
        return rows

    def gather_all(rows, events, even, *earlier):
        own = gather_rows(rows, far, events, *earlier)
        from_x, from_y = hop(own, across), hop(own, side)
        half = own.shape[0] // 2
        if even:
            corner = jnp.concatenate(
                [hop(from_y[:half], across), hop(from_x[half:], side)], axis=0
            )
        else:
            corner = hop(from_y, across)
        return own, from_x, from_y, corner

    def scatter_all(most, other_most, corner, other_corner, events, even, *earlier):
        corner = corner.astype(wider) + hop(other_corner, core, *earlier).astype(wider)
        corner = corner.astype(low)
        size = corner.shape[0]
        half = size // 2 if even else size
        for_y = hop(corner[:half], across)
        events.append(for_y)
        if n_all * 64 <= 4096:
            most = most.astype(wider) + hop(other_most, core, *earlier).astype(wider)
            own, sum_x, sum_y = (most[i * size : (i + 1) * size] for i in range(3))
        else:
            parts = [slice(i * size, (i + 1) * size) for i in range(3)]
            own, sum_x, sum_y = (
                most[rows].astype(wider) + hop(other_most[rows], core, *earlier).astype(wider)
                for rows in parts
            )
        if even:
            for_x = hop(corner[half:], side)
            sum_x = jnp.concatenate([sum_x[:half], sum_x[half:] + for_x.astype(wider)], axis=0)
            sum_y = jnp.concatenate([sum_y[:half] + for_y.astype(wider), sum_y[half:]], axis=0)
        else:
            sum_y = sum_y + for_y.astype(wider)
        moved_x, moved_y = hop(sum_x.astype(low), across), hop(sum_y.astype(low), side)
        events.append(moved_y)
        total = own + moved_x.astype(wider) + moved_y.astype(wider)
        return scatter_rows(total.astype(low), far[::-1], events)

    def local(
        x_prefix,
        x_action,
        cot_prefix,
        cot_action,
        prefix_block,
        action_block,
        valid_len,
        mix_weight,
        wq_prefix,
        wk_prefix,
        wv_prefix,
        wo_prefix,
        wg_prefix,
        wu_prefix,
        wd_prefix,
        norm1_prefix,
        norm2_prefix,
        wq_action,
        wk_action,
        wv_action,
        wo_action,
        wg_action,
        wu_action,
        wd_action,
        norm1_action,
        norm2_action,
    ):
        at = {"wide": lax.axis_index("wide"), "narrow": lax.axis_index("narrow")}
        head_dim = wk_prefix.shape[1]
        own = x_prefix.shape[0]
        width = x_prefix.shape[1]

        def streams(packed):
            return [packed[:, :width], packed[:, width:]]

        depth = [wg_prefix.shape[0], wg_action.shape[0]]
        units = [wg_prefix.shape[1] // n_wide, wg_action.shape[1] // n_wide]

        def fold(rows, lead):
            return jnp.concatenate(
                [rows[i * lead : (i + 1) * lead] for i in range(rows.shape[0] // lead)], axis=1
            )

        def unfold(rows, columns):
            return jnp.concatenate(
                [
                    rows[:, i * columns : (i + 1) * columns]
                    for i in range(rows.shape[1] // columns)
                ],
                axis=0,
            )

        def pack(parts):
            gate_p, up_p, down_p, gate_a, up_a, down_a = parts
            action = jnp.concatenate([gate_a, up_a, fold(down_a, depth[1])], axis=1)
            action = jnp.pad(action, [(0, 0), (0, units[0] - action.shape[1])])
            return jnp.concatenate([gate_p, up_p, fold(down_p, depth[0]), action], axis=0)

        def unpack(packet):
            d, f = depth[0], units[1]
            action = packet[3 * d :]
            return (
                packet[:d],
                packet[d : 2 * d],
                unfold(packet[2 * d : 3 * d], d),
                action[:, :f],
                action[:, f : 2 * f],
                unfold(action[:, 2 * f : 3 * f], depth[1]),
            )

        distances = list(range(1, n_wide))

        aligned = units[1] % 128 == 0 and depth[1] % 16 == 0 and units[1] == depth[1]
        folds = units[0] // depth[0]
        packet_shape = (3 * depth[0] + depth[1], units[0])
        peers = at["wide"] ^ jnp.arange(n_wide, dtype=jnp.int32)

        def packet_plan(outward, blocks_of):
            plan = []
            for k in range(n_wide):
                for array, array_at, packet_at in blocks_of(k):
                    if outward:
                        plan.append((array, array_at, k, lambda ref, at=packet_at: at))
                    else:
                        plan.append((k, lambda ref, at=packet_at: at, array, array_at))
            return plan

        def span(start, size):
            return slice(start, start + size)

        def packet_places(k, gate_at, up_at, down_at, arrays):
            for i, (d, f) in enumerate(zip(depth, units, strict=True)):
                gate, up, down = arrays[3 * i : 3 * i + 3]
                top = 3 * depth[0] if i else 0
                second = (span(top, d), span(f, f)) if i else (span(d, d), span(0, f))
                yield gate, functools.partial(gate_at, k, d, f), (span(top, d), span(0, f))
                yield up, functools.partial(up_at, k, d, f), second
                for part in range(f // d):
                    place = (span(top, d), span(2 * f, d)) if i else (span(2 * d, d), span(part * d, d))
                    yield down, functools.partial(down_at, k, d, f, part), place

        def weight_packet(k):
            peer = at["wide"] ^ k
            f, g = units
            return pack(
                (
                    lax.dynamic_slice_in_dim(wg_prefix, peer * f, f, 1),
                    lax.dynamic_slice_in_dim(wu_prefix, peer * f, f, 1),
                    lax.dynamic_slice_in_dim(wd_prefix, peer * f, f, 0),
                    lax.dynamic_slice_in_dim(wg_action, peer * g, g, 1),
                    lax.dynamic_slice_in_dim(wu_action, peer * g, g, 1),
                    lax.dynamic_slice_in_dim(wd_action, peer * g, g, 0),
                )
            )

        if aligned:
            packets = copy_blocks(
                packet_plan(
                    True,
                    lambda k: packet_places(
                        k,
                        lambda k, d, f, ref: (slice(None), block(ref[k], f)),
                        lambda k, d, f, ref: (slice(None), block(ref[k], f)),
                        lambda k, d, f, part, ref: (
                            pl.ds(pl.multiple_of(ref[k] * f, f) + part * d, d),
                            slice(None),
                        ),
                        range(6),
                    ),
                ),
                peers,
                [wg_prefix, wu_prefix, wd_prefix, wg_action, wu_action, wd_action],
                [packet_shape] * n_wide,
                "pack_weights",
            )
            packets = dict(enumerate(packets))
            weight_packet = packets.get
        else:
            packets = {0: weight_packet(0)}

        narrow_links = [across, core]
        x_packed = jnp.concatenate([x_prefix, x_action], axis=1)
        item_packed = gather_rows(x_packed, narrow_links)
        item_rows = streams(item_packed)

        gain_parts = [norm1_prefix, norm2_prefix, norm1_action, norm2_action]
        gain_sizes = [part.shape[0] for part in gain_parts]
        gain_stops = [sum(gain_sizes[: i + 1]) for i in range(4)]
        keyval_rows_of = [wk_prefix.shape[0], wk_action.shape[0]]
        gain_start = sum(keyval_rows_of)
        gain_rows = 16

        def pad_gains(row):
            return jnp.pad(
                row[..., None, :],
                [(0, 0)] * (row.ndim - 1) + [(0, gain_rows - 1), (0, 2 * head_dim - row.shape[-1])],
            )

        shared_events, query_events, out_events = [], [], []
        shared = gather_blocks(
            jnp.concatenate(
                [
                    jnp.concatenate([wk_prefix, wv_prefix], axis=1),
                    jnp.concatenate([wk_action, wv_action], axis=1),
                    pad_gains(jnp.concatenate(gain_parts)),
                ],
                axis=0,
            ),
            far + [side, across, core],
            at,
            shared_events,
        )
        gains_all = shared[:, gain_start, :].astype(wider)
        gains = [
            gains_all[:, stop - size : stop].reshape(-1)
            for stop, size in zip(gain_stops, gain_sizes, strict=True)
        ]
        first_gain = [gains[0], gains[2]]
        second_gain = [gains[1], gains[3]]
        keyval_weight = [
            shared[:, : keyval_rows_of[0]].reshape(-1, 2 * head_dim),
            shared[:, keyval_rows_of[0] : gain_start].reshape(-1, 2 * head_dim),
        ]
        query_depth = [wq_prefix.shape[0], wq_action.shape[0]]
        query_half = wq_prefix.shape[1] // 2
        query_packed = jnp.concatenate([wq_prefix, wq_action], axis=0)
        wide_links = far + [side]
        query_blocks = [
            gather_blocks(query_packed[:, :query_half], wide_links, at, []),
            gather_blocks(
                query_packed[:, query_half:],
                [side] + far,
                at,
                query_events,
                (),
                (packets[max(packets)],),
            ),
        ]
        query_weight = [
            [blocks[:, : query_depth[0]].reshape(-1, query_half) for blocks in query_blocks],
            [blocks[:, query_depth[0] :].reshape(-1, query_half) for blocks in query_blocks],
        ]
        out_blocks = gather_blocks(
            jnp.concatenate([wo_prefix.T, wo_action.T], axis=0),
            wide_links,
            at,
            out_events,
            (query_events[1],),
        )
        out_weight = [
            out_blocks[:, : query_depth[0]].reshape(-1, wo_prefix.shape[0]),
            out_blocks[:, query_depth[0] :].reshape(-1, wo_action.shape[0]),
        ]
        item_weight = mix_weight[0]
        dout = jnp.concatenate([cot_prefix, cot_action], axis=1).astype(wider) * item_weight
        grad_events = []
        grad_near = gather_all(dout.astype(low), grad_events, False, shared_events[-3])
        copying = n_all * own <= 4096
        if copying:
            grad_near = jnp.concatenate(grad_near, axis=0)
            grad_far = hop(grad_near, core)
            grad_near, grad_far = ([(rows, i) for i in range(4)] for rows in (grad_near, grad_far))
        else:
            grad_far = [(hop(rows, core), 0) for rows in grad_near]
            grad_near = [(rows, 0) for rows in grad_near]
        def send_packets(few, packet_of, *earlier):
            for k in few:
                packets[k] = hop(packet_of(k), ("wide", k), *earlier)

        def share(first, last):
            return [k for k in distances if first * n_wide <= 8 * k < last * n_wide]

        send_packets(share(4, 5), weight_packet, query_events[0])
        send_packets(share(6, 7), weight_packet, shared_events[-2])
        send_packets(share(2, 3), weight_packet, shared_events[-2])

        all_normed = [
            rms_norm(item_rows[stream].astype(wider), first_gain[stream]).astype(low)
            for stream in range(2)
        ]
        prefix_len = item_packed.shape[0]
        total_rows = 2 * prefix_len
        joined = jnp.concatenate(
            [
                product(all_normed[stream], keyval_weight[stream]).astype(low)
                for stream in range(2)
            ],
            axis=0,
        )
        key_rows = joined[:, :head_dim]
        values = joined[:, head_dim:]
        queries = jnp.concatenate(
            [
                jnp.concatenate(
                    [
                        (product(all_normed[stream], part) * scaling).astype(low)
                        for part in query_weight[stream]
                    ],
                    axis=1,
                )
                for stream in range(2)
            ],
            axis=0,
        ).reshape(total_rows, -1, head_dim)
        offsets = [0]
        for unused, mask in narrow_links:
            offsets = offsets + [offset ^ mask for offset in offsets]
        owners = at["narrow"] ^ jnp.array(offsets, jnp.int32)

        def reorder(ids):
            return jnp.take(ids.reshape(n_narrow, -1), owners, axis=0).reshape(-1)

        blocks = jnp.concatenate(
            [reorder(prefix_block[0]), reorder(action_block[0]) + PREFIX_BLOCKS]
        )
        positions = (owners[:, None] * own + jnp.arange(own, dtype=jnp.int32)[None]).reshape(-1)
        usable = jnp.concatenate(
            [
                positions < valid_len[0],
                jnp.ones((total_rows - prefix_len,), dtype=jnp.bool_),
            ]
        )
        allowed = (blocks[None, :] <= blocks[:, None]) & usable[None, :]
        scores = masked_scores(queries, key_rows, allowed)
        highest = jnp.max(scores, axis=-1, keepdims=True)
        exponent = jnp.exp(scores - highest)
        denominator = jnp.sum(exponent, axis=-1, keepdims=True)
        log_total = highest + jnp.log(denominator)
        attention = (exponent / denominator).astype(low)
        mixed_all = jnp.einsum("hqk,kd->qhd", attention, values, preferred_element_type=wider)
        mixed_all = mixed_all.astype(low).reshape(total_rows, -1)
        mixed_rows = [mixed_all[:prefix_len], mixed_all[prefix_len:]]
        attended_all = (
            jnp.concatenate(
                [
                    cols_contract(mixed_rows[stream], out_weight[stream]).astype(low)
                    for stream in range(2)
                ],
                axis=1,
            )
        )
        attended_events = []
        attended_all = tie(attended_all, packets[n_wide // 2], *grad_events)
        attended = scatter_rows(attended_all, [core, across], attended_events)
        send_packets(share(7, 8), weight_packet, attended_events[1])
        send_packets(share(3, 4), weight_packet, attended_events[1])
        inputs = [x_prefix.astype(wider), x_action.astype(wider)]
        middle = [
            rows + part for rows, part in zip(inputs, streams(attended), strict=True)
        ]
        normed2 = jnp.concatenate(
            [rms_norm(middle[stream], second_gain[stream]).astype(low) for stream in range(2)],
            axis=1,
        )
        token_events = []
        normed2 = tie(normed2, *(packets[k] for k in share(6, 7) + share(2, 3)))
        near = gather_all(normed2, token_events, True)
        if copying:
            other_most = hop(jnp.concatenate(near[:3], axis=0), core)
            token_far = [(other_most, i) for i in range(3)] + [(hop(near[3], core), 0)]
        else:
            token_far = [(hop(rows, core), 0) for rows in near]
        send_packets(share(5, 6), weight_packet, token_events[-1])
        send_packets(share(0, 2), weight_packet, token_events[-1])
        if aligned:
            feed_weights = copy_blocks(
                packet_plan(
                    False,
                    lambda k: packet_places(
                        k,
                        lambda k, d, f, ref: (block(ref[k], d), span(0, f)),
                        lambda k, d, f, ref: (block(ref[k], d), span(f, f)),
                        lambda k, d, f, part, ref: (span(part * d, d), block(ref[k], d)),
                        (0, 0, 1, 2, 2, 3),
                    ),
                ),
                peers,
                [packets[k] for k in range(n_wide)],
                [
                    (depth[0] * n_wide, 2 * units[0]),
                    (units[0], depth[0] * n_wide),
                    (depth[1] * n_wide, 2 * units[1]),
                    (units[1], depth[1] * n_wide),
                ],
                "unpack_weights",
            )
        else:
            gate_up_weight = [jnp.zeros((depth[i] * n_wide, 2 * units[i]), low) for i in range(2)]
            down_weight = [jnp.zeros((units[i], depth[i] * n_wide), low) for i in range(2)]
            for k, packet in packets.items():
                peer = at["wide"] ^ k
                parts = unpack(packet)
                for i in range(2):
                    gate_up_weight[i] = lax.dynamic_update_slice_in_dim(
                        gate_up_weight[i],
                        jnp.concatenate(parts[3 * i : 3 * i + 2], axis=1),
                        peer * depth[i],
                        0,
                    )
                    down_weight[i] = lax.dynamic_update_slice_in_dim(
                        down_weight[i], parts[3 * i + 2], peer * depth[i], 1
                    )
            feed_weights = [gate_up_weight[0], down_weight[0], gate_up_weight[1], down_weight[1]]

        size = near[0].shape[0]
        feed = functools.partial(
            feed_forward,
            weights=feed_weights,
            size=size,
            total=n_all * own,
            n_copied=4 if copying else 0,
        )
        token_pieces = [(rows, 0) for rows in near] + [token_far[3], *token_far[:3]]
        grad_pieces = [*grad_near, grad_far[3], *grad_far[:3]]
        kept, back_most, out_most = feed(token_pieces[:3], grad_pieces[:3], kept=[], first=0)
        kept, back_corner, out_corner = feed(
            token_pieces[3:5], grad_pieces[3:5], kept=kept, first=3
        )
        kept, back_far, out_far = feed(token_pieces[5:], grad_pieces[5:], kept=kept, first=5)
        hidden_rows, both_rows = kept[-4::2], kept[-3::2]
        if not copying:
            gate_up_grad = [0.0, 0.0]
            down_grad = [0.0, 0.0]
            for i, ((token, token_at), (grad, grad_at)) in enumerate(
                zip(token_pieces, grad_pieces, strict=True)
            ):
                rows = slice(i * size, (i + 1) * size)
                token = streams(token[token_at * size : (token_at + 1) * size])
                grad = streams(grad[grad_at * size : (grad_at + 1) * size])
                for j in range(2):
                    gate_up_grad[j] = gate_up_grad[j] + rows_contract(token[j], both_rows[j][rows])
                    down_grad[j] = down_grad[j] + rows_contract(hidden_rows[j][rows], grad[j])
            gate_up_grad = [grad.astype(low) for grad in gate_up_grad]
            down_grad = [grad.astype(low) for grad in down_grad]
            back_corner, back_far, out_corner, out_far, *held = join(
                back_corner, back_far, out_corner, out_far, *gate_up_grad, *down_grad
            )
            gate_up_grad, down_grad = held[:2], held[2:]
        back_events = []
        dnormed2_packed = scatter_all(
            back_most, back_far, back_corner[:size], back_corner[size:], back_events, True
        )
        dnormed2 = streams(dnormed2_packed)
        mlp_out = streams(
            scatter_all(
                out_most, out_far, out_corner[:size], out_corner[size:], [], False, back_events[-1]
            )
        )
        if copying:
            gate_up_grad = [rows_contract(kept[i], both_rows[i]) for i in range(2)]
            down_grad = [rows_contract(hidden_rows[i], kept[2 + i]) for i in range(2)]
            gate_up_grad = [grad.astype(low) for grad in gate_up_grad]
            down_grad = [grad.astype(low) for grad in down_grad]

        def gradient_packet(k):
            peer = at["wide"] ^ k
            parts = []
            for i in range(2):
                both = lax.dynamic_slice_in_dim(gate_up_grad[i], peer * depth[i], depth[i], 0)
                down = lax.dynamic_slice_in_dim(down_grad[i], peer * depth[i], depth[i], 1)
                parts += [both[:, : units[i]], both[:, units[i] :], down]
            return pack(parts)

        if aligned:
            packets = copy_blocks(
                packet_plan(
                    True,
                    lambda k: packet_places(
                        k,
                        lambda k, d, f, ref: (block(ref[k], d), span(0, f)),
                        lambda k, d, f, ref: (block(ref[k], d), span(f, f)),
                        lambda k, d, f, part, ref: (span(part * d, d), block(ref[k], d)),
                        (0, 0, 1, 2, 2, 3),
                    ),
                ),
                peers,
                [gate_up_grad[0], down_grad[0], gate_up_grad[1], down_grad[1]],
                [packet_shape] * n_wide,
                "pack_gradients",
            )
            packets = dict(enumerate(packets))
            gradient_packet = packets.get
        else:
            packets = {0: gradient_packet(0)}
        send_packets(share(4, 5), gradient_packet)
        send_packets(share(2, 3), gradient_packet)
        send_packets(share(6, 7), gradient_packet, back_events[1])
        send_packets(share(0, 2), gradient_packet, back_events[-1])
        send_packets(share(5, 6), gradient_packet, back_events[-1])
        outputs = [(middle[stream] + mlp_out[stream]).astype(low) for stream in range(2)]
        dmiddle = []
        grad_second = []
        for stream, dout_part in enumerate(streams(dout)):
            from_norm, gain_part = norm_back(middle[stream], second_gain[stream], dnormed2[stream])
            dmiddle.append(dout_part + from_norm)
            grad_second.append(gain_part)
        att_events = []
        grad_att = streams(
            gather_rows(
                tie(
                    jnp.concatenate([part.astype(low) for part in dmiddle], axis=1),
                    *(packets[k] for k in share(4, 5) + share(2, 3)),
                ),
                narrow_links,
                att_events,
            )
        )
        send_packets(share(7, 8), gradient_packet, att_events[0])
        send_packets(share(3, 4), gradient_packet, att_events[0])

        def return_wide(parts, links):
            blocks = jnp.concatenate(
                [part.astype(low).reshape(n_wide, -1, part.shape[1]) for part in parts], axis=1
            )
            return scatter_blocks(blocks, links, at)

        out_grads = return_wide(
            [rows_contract(grad_att[stream], mixed_rows[stream]) for stream in range(2)],
            wide_links[::-1],
        )
        grad_out_w = [out_grads[: query_depth[0]].T, out_grads[query_depth[0] :].T]
        dmixed = jnp.concatenate(
            [product(grad_att[stream], out_weight[stream]) for stream in range(2)],
            axis=0,
        )
        dmixed = dmixed.astype(low).reshape(total_rows, -1, head_dim)
        recomputed = jnp.exp(masked_scores(queries, key_rows, allowed) - log_total)
        dprobs = jnp.einsum("qhd,kd->hqk", dmixed, values, preferred_element_type=wider)
        row_inner = jnp.sum(recomputed * dprobs, axis=-1, keepdims=True)
        dscores = (recomputed * (dprobs - row_inner)).astype(low)
        dquery = jnp.einsum("hqk,kd->qhd", dscores, key_rows, preferred_element_type=wider)
        dquery = (dquery.astype(low) * scaling).reshape(total_rows, -1)
        grad_key = jnp.einsum("hqk,qhd->kd", dscores, queries, preferred_element_type=wider)
        dvalue = jnp.einsum(
            "hqk,qhd->kd", recomputed.astype(low), dmixed, preferred_element_type=wider
        )
        grad_keyval = jnp.concatenate([grad_key, dvalue], axis=1).astype(low)
        dquery_rows = [dquery[:prefix_len], dquery[prefix_len:]]
        keyval_rows = [grad_keyval[:prefix_len], grad_keyval[prefix_len:]]
        query_links = [[side] + far[::-1], far[::-1] + [side]]
        query_grads = jnp.concatenate(
            [
                return_wide(
                    [
                        rows_contract(
                            all_normed[stream],
                            dquery_rows[stream][:, part * query_half : (part + 1) * query_half],
                        )
                        for stream in range(2)
                    ],
                    query_links[part],
                )
                for part in range(2)
            ],
            axis=1,
        )
        grad_query_w = [query_grads[: query_depth[0]], query_grads[query_depth[0] :]]
        wide_mlp = []
        for i, (gate_w, down_w) in enumerate(((wg_prefix, wd_prefix), (wg_action, wd_action))):
            wide_mlp += [
                jnp.zeros(gate_w.shape, wider),
                jnp.zeros(gate_w.shape, wider),
                jnp.zeros(down_w.shape, wider),
            ]
        for k, packet in packets.items():
            peer = at["wide"] ^ k
            parts = unpack(packet)
            for i in range(6):
                wide_mlp[i] = lax.dynamic_update_slice_in_dim(
                    wide_mlp[i],
                    parts[i].astype(wider),
                    peer * units[i // 3],
                    0 if i % 3 == 2 else 1,
                )

        dnormed_parts = []
        grad_first = []
        for stream in range(2):
            dnormed = cols_contract(keyval_rows[stream], keyval_weight[stream])
            for part in range(2):
                dnormed = dnormed + cols_contract(
                    dquery_rows[stream][:, part * query_half : (part + 1) * query_half],
                    query_weight[stream][part],
                )
            wide_rows = item_rows[stream].astype(wider)
            unit_rows = wide_rows * lax.rsqrt(
                jnp.mean(wide_rows * wide_rows, axis=-1, keepdims=True) + epsilon
            )
            grad_first.append(jnp.sum(dnormed * unit_rows, axis=0))
            dnormed_parts.append(dnormed.astype(low))
        dnormed = streams(
            scatter_rows(jnp.concatenate(dnormed_parts, axis=1), [core, across])
        )
        grad_inputs = [
            dmiddle[stream] + norm_back(inputs[stream], first_gain[stream], dnormed[stream])[0]
            for stream in range(2)
        ]
        gain_grads = jnp.concatenate(
            [
                part.reshape(n_all, -1)
                for part in (grad_first[0], grad_second[0], grad_first[1], grad_second[1])
            ],
            axis=1,
        )
        shared_grads = scatter_blocks(
            jnp.concatenate(
                [
                    rows_contract(all_normed[stream], keyval_rows[stream])
                    .astype(low)
                    .reshape(n_all, -1, 2 * head_dim)
                    for stream in range(2)
                ]
                + [pad_gains(gain_grads.astype(low))],
                axis=1,
            ),
            [core, across, side] + far[::-1],
            at,
        )
        grad_keyval_w = [
            shared_grads[: keyval_rows_of[0]],
            shared_grads[keyval_rows_of[0] : gain_start],
        ]
        gain_grads = shared_grads[gain_start]
        small = [
            gain_grads[stop - size : stop]
            for stop, size in zip(gain_stops, gain_sizes, strict=True)
        ]
        weights = [
            (
                grad_query_w[i],
                grad_keyval_w[i][:, :head_dim],
                grad_keyval_w[i][:, head_dim:],
                grad_out_w[i],
                *wide_mlp[3 * i : 3 * i + 3],
                small[2 * i],
                small[2 * i + 1],
            )
            for i in range(2)
        ]
        return (*outputs, *grad_inputs, *weights[0], *weights[1])

    return local


def solution(mesh):
    rows = P(BOTH, None)
    block = P("wide", "narrow")
    turned = P("narrow", "wide")
    vector = P(BOTH)
    weights = (block, rows, rows, turned, block, block, turned, vector, vector)
    return jax.shard_map(
        make_local(mesh.shape["wide"], mesh.shape["narrow"]),
        mesh=mesh,
        in_specs=(
            rows,
            rows,
            rows,
            rows,
            P("wide", None),
            P("wide", None),
            P("wide"),
            P("wide"),
            *weights,
            *weights,
        ),
        out_specs=(rows, rows, rows, rows, *weights, *weights),
        check_vma=False,
    )
```

```python
import functools

import jax
import jax.numpy as jnp
from jax import lax
from jax.experimental import pallas as pl
from jax.experimental.pallas import tpu as pltpu
from jax.sharding import PartitionSpec as P

PREFIX_BLOCKS = 4
BOTH = ("wide", "narrow")

epsilon = 1e-06
scaling = 0.0625
masked_score = -1e30
low = jnp.bfloat16
wider = jnp.float32


def rms_norm(features, weight):
    return (
        features
        * lax.rsqrt(jnp.mean(features * features, axis=-1, keepdims=True) + epsilon)
        * weight
    )


def product(former, latter):
    return jnp.dot(former, latter, preferred_element_type=wider)


def rows_contract(former, latter):
    return lax.dot_general(
        former, latter, (((0,), (0,)), ((), ())), preferred_element_type=wider
    )


def cols_contract(former, latter):
    return lax.dot_general(
        former, latter, (((1,), (1,)), ((), ())), preferred_element_type=wider
    )


def norm_back(features, weight, upstream):
    unused, pullback = jax.vjp(rms_norm, features, weight)
    return pullback(upstream)


def tie(value, *earlier):
    return lax.optimization_barrier((value, *earlier))[0] if earlier else value


def masked_scores(queries, key_rows, allowed):
    scores = jnp.einsum("qhd,kd->hqk", queries, key_rows, preferred_element_type=wider)
    return jnp.where(allowed[None], scores, masked_score)


def copies_kernel(plan, n_in, place_ref, *refs):
    copied = refs[-1]
    copies = []
    for i, (source, source_at, target, target_at) in enumerate(plan):
        source_ref = refs[source].at[source_at(place_ref)]
        target_ref = refs[n_in + target].at[target_at(place_ref)]
        copies.append(pltpu.make_async_copy(source_ref, target_ref, copied.at[i]))
    for copy in copies:
        copy.start()
    for copy in copies:
        copy.wait()


def copy_blocks(plan, places, arrays, shapes, name):
    any_spec = pl.BlockSpec(memory_space=pl.ANY)
    moved = 2 * sum(shape[0] * shape[1] * 2 for shape in shapes)
    return pl.pallas_call(
        functools.partial(copies_kernel, plan, len(arrays)),
        in_specs=[pl.BlockSpec(memory_space=pltpu.SMEM)] + [any_spec] * len(arrays),
        out_specs=[pl.BlockSpec(memory_space=pltpu.VMEM)] * len(shapes),
        scratch_shapes=[pltpu.SemaphoreType.DMA((len(plan),))],
        compiler_params=pltpu.CompilerParams(vmem_limit_bytes=24 << 20),
        out_shape=[jax.ShapeDtypeStruct(shape, low) for shape in shapes],
        cost_estimate=pl.CostEstimate(flops=0, bytes_accessed=moved, transcendentals=0),
        name=name,
    )(places, *arrays)


def block(index, size):
    return pl.ds(pl.multiple_of(index * size, size), size)


def feed_kernel(count, half, n_kept, n_copied, first, *refs):
    token_refs, refs = refs[:count], refs[count:]
    grad_refs, refs = refs[:count], refs[count:]
    weight_refs, refs = refs[:4], refs[4 + n_kept :]
    kept_refs, row_refs = refs[:n_copied], refs[n_copied : n_copied + 4]
    back_ref, out_ref, copied = refs[n_copied + 4 :]
    step = pl.program_id(0)
    tile = token_refs[0].shape[0]
    width = weight_refs[1].shape[1]
    columns_of = (slice(0, width), slice(width, width + weight_refs[3].shape[1]))
    slope = 0.7978845608028654

    def run(token_ref, grad_ref):
        place = block(first + step, tile)
        copies = [
            pltpu.make_async_copy(
                source.at[:, columns_of[i % 2]], kept_refs[i].at[place], copied.at[i]
            )
            for i, source in enumerate((token_ref, token_ref, grad_ref, grad_ref)[:n_copied])
        ]
        for copy in copies:
            copy.start()
        for i, columns in enumerate(columns_of):
            gate_up_ref, down_ref = weight_refs[2 * i : 2 * i + 2]
            hidden_ref, both_ref = row_refs[2 * i : 2 * i + 2]
            units = down_ref.shape[0]
            both = product(token_ref[:, columns], gate_up_ref[...])
            gate, up = both[:, :units], both[:, units:]
            square = gate * gate
            bend = jnp.tanh(slope * gate * (1.0 + 0.044715 * square))
            active = 0.5 * gate * (1.0 + bend)
            hidden = (active * up).astype(low)
            hidden_ref[...] = hidden
            dhidden = cols_contract(grad_ref[:, columns], down_ref[...])
            steep = 0.5 * (1.0 + bend) + 0.5 * gate * (1.0 - bend * bend) * slope * (
                1.0 + 3 * 0.044715 * square
            )
            both_ref[:, :units] = (dhidden * up * steep).astype(low)
            both_ref[:, units:] = (dhidden * active).astype(low)
            back_ref[:, columns] = cols_contract(both_ref[...], gate_up_ref[...]).astype(low)
            out_ref[:, columns] = product(hidden, down_ref[...]).astype(low)
        for copy in copies:
            copy.wait()

    for piece in range(count):
        pl.when(step // half == piece)(
            functools.partial(run, token_refs[piece], grad_refs[piece])
        )


def feed_forward(tokens, grads, weights, kept, size, total, first, n_copied):
    count = len(tokens)
    columns = tokens[0][0].shape[1]
    tile = min(size, 256)
    half = size // tile
    units = [weights[1].shape[0], weights[3].shape[0]]
    widths = [weights[1].shape[1], weights[3].shape[1]]
    first = first * half
    rows = [units[0], 2 * units[0], units[1], 2 * units[1]]
    any_spec = pl.BlockSpec(memory_space=pl.ANY)

    def piece_spec(piece, place):
        return pl.BlockSpec(
            (tile, columns),
            lambda i: (place * half + jnp.clip(i - piece * half, 0, half - 1), 0),
        )

    out = pl.pallas_call(
        functools.partial(feed_kernel, count, half, len(kept), n_copied, first),
        grid=(count * half,),
        in_specs=[piece_spec(i, place) for i, (unused, place) in enumerate(tokens)]
        + [piece_spec(i, place) for i, (unused, place) in enumerate(grads)]
        + [
            pl.BlockSpec(w.shape, lambda i: (0, 0), pipeline_mode=pl.Buffered(1)) for w in weights
        ]
        + [any_spec] * len(kept),
        out_specs=[any_spec] * n_copied
        + [pl.BlockSpec((tile, w), lambda i: (first + i, 0)) for w in rows]
        + [pl.BlockSpec((tile, columns), lambda i: (i, 0))] * 2,
        scratch_shapes=[pltpu.SemaphoreType.DMA((4,))],
        out_shape=[
            jax.ShapeDtypeStruct((total, w), low) for w in (widths * 2)[:n_copied] + rows
        ]
        + [jax.ShapeDtypeStruct((count * size, columns), low)] * 2,
        input_output_aliases={2 * count + 4 + i: i for i in range(len(kept))},
        compiler_params=pltpu.CompilerParams(vmem_limit_bytes=52 << 20),
        cost_estimate=pl.CostEstimate(
            flops=2 * count * size * 6 * (widths[0] * units[0] + widths[1] * units[1]),
            bytes_accessed=12 * count * size * columns,
            transcendentals=0,
        ),
        name="feed_forward",
    )(*(array for array, unused in tokens), *(array for array, unused in grads), *weights, *kept)
    return out[: n_copied + 4], out[n_copied + 4], out[n_copied + 5]


def make_local(n_wide, n_narrow):
    n_all = n_wide * n_narrow
    wide_masks = [1 << bit for bit in range(n_wide.bit_length() - 1)]
    far = [("wide", mask) for mask in wide_masks[:0:-1]]
    side, across, core = ("wide", 1), ("narrow", 2), ("narrow", 1)
    sizes = {"wide": n_wide, "narrow": n_narrow}

    def join(*values):
        return lax.optimization_barrier(values)

    def hop(value, link, *earlier):
        axis, mask = link
        value = tie(value, *earlier)
        return lax.ppermute(value, axis, [(i, i ^ mask) for i in range(sizes[axis])])

    def rank_of(link):
        return link[1] if link[0] == "narrow" else link[1] * n_narrow

    def gather_blocks(block, links, at, events, *earlier):
        held = []
        for i, link in enumerate(links):
            position = sum(other > rank_of(link) for other in held)
            moved = hop(block, link, *(earlier[i] if i < len(earlier) else ()))
            events.append(moved)
            block = jnp.where(
                (at[link[0]] & link[1]) != 0,
                jnp.stack([moved, block], position),
                jnp.stack([block, moved], position),
            )
            held.append(rank_of(link))
        return block.reshape(-1, *block.shape[len(links) :])

    def scatter_blocks(blocks, links, at):
        held = sorted((rank_of(link) for link in links), reverse=True)
        blocks = blocks.reshape(*(2 for unused in links), *blocks.shape[1:])
        for stage, link in enumerate(links):
            position = held.index(rank_of(link))
            bit = jnp.minimum(at[link[0]] & link[1], 1)
            mine = lax.dynamic_index_in_dim(blocks, bit, position, keepdims=False)
            theirs = lax.dynamic_index_in_dim(blocks, 1 - bit, position, keepdims=False)
            blocks = mine.astype(wider) + hop(theirs, link).astype(wider)
            if stage + 1 < len(links):
                blocks = blocks.astype(low)
            held.remove(rank_of(link))
        return blocks

    def gather_rows(rows, links, events=None, *earlier):
        for link in links:
            moved = hop(rows, link, *earlier)
            earlier = ()
            if events is not None:
                events.append(moved)
            rows = jnp.concatenate([rows, moved], axis=0)
        return rows

    def scatter_rows(rows, links, events=None):
        for stage, link in enumerate(links):
            half = rows.shape[0] // 2
            moved = hop(rows[half:], link)
            if events is not None:
                events.append(moved)
            rows = rows[:half].astype(wider) + moved.astype(wider)
            if stage + 1 < len(links):
                rows = rows.astype(low)
        return rows

    def gather_all(rows, events, even, *earlier):
        own = gather_rows(rows, far, events, *earlier)
        from_x, from_y = hop(own, across), hop(own, side)
        half = own.shape[0] // 2
        if even:
            corner = jnp.concatenate(
                [hop(from_y[:half], across), hop(from_x[half:], side)], axis=0
            )
        else:
            corner = hop(from_y, across)
        return own, from_x, from_y, corner

    def scatter_all(most, other_most, corner, other_corner, events, even, *earlier):
        corner = corner.astype(wider) + hop(other_corner, core, *earlier).astype(wider)
        corner = corner.astype(low)
        size = corner.shape[0]
        half = size // 2 if even else size
        for_y = hop(corner[:half], across)
        events.append(for_y)
        if n_all * 64 <= 4096:
            most = most.astype(wider) + hop(other_most, core, *earlier).astype(wider)
            own, sum_x, sum_y = (most[i * size : (i + 1) * size] for i in range(3))
        else:
            parts = [slice(i * size, (i + 1) * size) for i in range(3)]
            own, sum_x, sum_y = (
                most[rows].astype(wider) + hop(other_most[rows], core, *earlier).astype(wider)
                for rows in parts
            )
        if even:
            for_x = hop(corner[half:], side)
            sum_x = jnp.concatenate([sum_x[:half], sum_x[half:] + for_x.astype(wider)], axis=0)
            sum_y = jnp.concatenate([sum_y[:half] + for_y.astype(wider), sum_y[half:]], axis=0)
        else:
            sum_y = sum_y + for_y.astype(wider)
        moved_x, moved_y = hop(sum_x.astype(low), across), hop(sum_y.astype(low), side)
        events.append(moved_y)
        total = own + moved_x.astype(wider) + moved_y.astype(wider)
        return scatter_rows(total.astype(low), far[::-1], events)

    def local(
        x_prefix,
        x_action,
        cot_prefix,
        cot_action,
        prefix_block,
        action_block,
        valid_len,
        mix_weight,
        wq_prefix,
        wk_prefix,
        wv_prefix,
        wo_prefix,
        wg_prefix,
        wu_prefix,
        wd_prefix,
        norm1_prefix,
        norm2_prefix,
        wq_action,
        wk_action,
        wv_action,
        wo_action,
        wg_action,
        wu_action,
        wd_action,
        norm1_action,
        norm2_action,
    ):
        at = {"wide": lax.axis_index("wide"), "narrow": lax.axis_index("narrow")}
        head_dim = wk_prefix.shape[1]
        own = x_prefix.shape[0]
        width = x_prefix.shape[1]

        def streams(packed):
            return [packed[:, :width], packed[:, width:]]

        depth = [wg_prefix.shape[0], wg_action.shape[0]]
        units = [wg_prefix.shape[1] // n_wide, wg_action.shape[1] // n_wide]

        def fold(rows, lead):
            return jnp.concatenate(
                [rows[i * lead : (i + 1) * lead] for i in range(rows.shape[0] // lead)], axis=1
            )

        def unfold(rows, columns):
            return jnp.concatenate(
                [
                    rows[:, i * columns : (i + 1) * columns]
                    for i in range(rows.shape[1] // columns)
                ],
                axis=0,
            )

        def pack(parts):
            gate_p, up_p, down_p, gate_a, up_a, down_a = parts
            action = jnp.concatenate([gate_a, up_a, fold(down_a, depth[1])], axis=1)
            action = jnp.pad(action, [(0, 0), (0, units[0] - action.shape[1])])
            return jnp.concatenate([gate_p, up_p, fold(down_p, depth[0]), action], axis=0)

        def unpack(packet):
            d, f = depth[0], units[1]
            action = packet[3 * d :]
            return (
                packet[:d],
                packet[d : 2 * d],
                unfold(packet[2 * d : 3 * d], d),
                action[:, :f],
                action[:, f : 2 * f],
                unfold(action[:, 2 * f : 3 * f], depth[1]),
            )

        distances = list(range(1, n_wide))

        aligned = units[1] % 128 == 0 and depth[1] % 16 == 0 and units[1] == depth[1]
        folds = units[0] // depth[0]
        packet_shape = (3 * depth[0] + depth[1], units[0])
        peers = at["wide"] ^ jnp.arange(n_wide, dtype=jnp.int32)

        def packet_plan(outward, blocks_of):
            plan = []
            for k in range(n_wide):
                for array, array_at, packet_at in blocks_of(k):
                    if outward:
                        plan.append((array, array_at, k, lambda ref, at=packet_at: at))
                    else:
                        plan.append((k, lambda ref, at=packet_at: at, array, array_at))
            return plan

        def span(start, size):
            return slice(start, start + size)

        def packet_places(k, gate_at, up_at, down_at, arrays):
            for i, (d, f) in enumerate(zip(depth, units, strict=True)):
                gate, up, down = arrays[3 * i : 3 * i + 3]
                top = 3 * depth[0] if i else 0
                second = (span(top, d), span(f, f)) if i else (span(d, d), span(0, f))
                yield gate, functools.partial(gate_at, k, d, f), (span(top, d), span(0, f))
                yield up, functools.partial(up_at, k, d, f), second
                for part in range(f // d):
                    place = (span(top, d), span(2 * f, d)) if i else (span(2 * d, d), span(part * d, d))
                    yield down, functools.partial(down_at, k, d, f, part), place

        def weight_packet(k):
            peer = at["wide"] ^ k
            f, g = units
            return pack(
                (
                    lax.dynamic_slice_in_dim(wg_prefix, peer * f, f, 1),
                    lax.dynamic_slice_in_dim(wu_prefix, peer * f, f, 1),
                    lax.dynamic_slice_in_dim(wd_prefix, peer * f, f, 0),
                    lax.dynamic_slice_in_dim(wg_action, peer * g, g, 1),
                    lax.dynamic_slice_in_dim(wu_action, peer * g, g, 1),
                    lax.dynamic_slice_in_dim(wd_action, peer * g, g, 0),
                )
            )

        if aligned:
            packets = copy_blocks(
                packet_plan(
                    True,
                    lambda k: packet_places(
                        k,
                        lambda k, d, f, ref: (slice(None), block(ref[k], f)),
                        lambda k, d, f, ref: (slice(None), block(ref[k], f)),
                        lambda k, d, f, part, ref: (
                            pl.ds(pl.multiple_of(ref[k] * f, f) + part * d, d),
                            slice(None),
                        ),
                        range(6),
                    ),
                ),
                peers,
                [wg_prefix, wu_prefix, wd_prefix, wg_action, wu_action, wd_action],
                [packet_shape] * n_wide,
                "pack_weights",
            )
            packets = dict(enumerate(packets))
            weight_packet = packets.get
        else:
            packets = {0: weight_packet(0)}

        narrow_links = [across, core]
        x_packed = jnp.concatenate([x_prefix, x_action], axis=1)
        item_packed = gather_rows(x_packed, narrow_links)
        item_rows = streams(item_packed)

        gain_parts = [norm1_prefix, norm2_prefix, norm1_action, norm2_action]
        gain_sizes = [part.shape[0] for part in gain_parts]
        gain_stops = [sum(gain_sizes[: i + 1]) for i in range(4)]
        keyval_rows_of = [wk_prefix.shape[0], wk_action.shape[0]]
        gain_start = sum(keyval_rows_of)
        gain_rows = 16

        def pad_gains(row):
            return jnp.pad(
                row[..., None, :],
                [(0, 0)] * (row.ndim - 1) + [(0, gain_rows - 1), (0, 2 * head_dim - row.shape[-1])],
            )

        shared_events, query_events, out_events = [], [], []
        shared = gather_blocks(
            jnp.concatenate(
                [
                    jnp.concatenate([wk_prefix, wv_prefix], axis=1),
                    jnp.concatenate([wk_action, wv_action], axis=1),
                    pad_gains(jnp.concatenate(gain_parts)),
                ],
                axis=0,
            ),
            far + [side, across, core],
            at,
            shared_events,
        )
        gains_all = shared[:, gain_start, :].astype(wider)
        gains = [
            gains_all[:, stop - size : stop].reshape(-1)
            for stop, size in zip(gain_stops, gain_sizes, strict=True)
        ]
        first_gain = [gains[0], gains[2]]
        second_gain = [gains[1], gains[3]]
        keyval_weight = [
            shared[:, : keyval_rows_of[0]].reshape(-1, 2 * head_dim),
            shared[:, keyval_rows_of[0] : gain_start].reshape(-1, 2 * head_dim),
        ]
        query_depth = [wq_prefix.shape[0], wq_action.shape[0]]
        query_half = wq_prefix.shape[1] // 2
        query_packed = jnp.concatenate([wq_prefix, wq_action], axis=0)
        wide_links = far + [side]
        query_blocks = [
            gather_blocks(query_packed[:, :query_half], wide_links, at, []),
            gather_blocks(
                query_packed[:, query_half:],
                [side] + far,
                at,
                query_events,
                (),
                (packets[max(packets)],),
            ),
        ]
        query_weight = [
            [blocks[:, : query_depth[0]].reshape(-1, query_half) for blocks in query_blocks],
            [blocks[:, query_depth[0] :].reshape(-1, query_half) for blocks in query_blocks],
        ]
        out_blocks = gather_blocks(
            jnp.concatenate([wo_prefix.T, wo_action.T], axis=0),
            wide_links,
            at,
            out_events,
            (query_events[1],),
        )
        out_weight = [
            out_blocks[:, : query_depth[0]].reshape(-1, wo_prefix.shape[0]),
            out_blocks[:, query_depth[0] :].reshape(-1, wo_action.shape[0]),
        ]
        item_weight = mix_weight[0]
        dout = jnp.concatenate([cot_prefix, cot_action], axis=1).astype(wider) * item_weight
        grad_events = []
        grad_near = gather_all(dout.astype(low), grad_events, False, shared_events[-3])
        copying = n_all * own <= 4096
        if copying:
            grad_near = jnp.concatenate(grad_near, axis=0)
            grad_far = hop(grad_near, core)
            grad_near, grad_far = ([(rows, i) for i in range(4)] for rows in (grad_near, grad_far))
        else:
            grad_far = [(hop(rows, core), 0) for rows in grad_near]
            grad_near = [(rows, 0) for rows in grad_near]
        def send_packets(few, packet_of, *earlier):
            for k in few:
                packets[k] = hop(packet_of(k), ("wide", k), *earlier)

        def share(first, last):
            return [k for k in distances if first * n_wide <= 8 * k < last * n_wide]

        send_packets(share(4, 5), weight_packet, query_events[0])
        send_packets(share(6, 7), weight_packet, shared_events[-2])
        send_packets(share(2, 3), weight_packet, shared_events[-2])

        all_normed = [
            rms_norm(item_rows[stream].astype(wider), first_gain[stream]).astype(low)
            for stream in range(2)
        ]
        prefix_len = item_packed.shape[0]
        total_rows = 2 * prefix_len
        joined = jnp.concatenate(
            [
                product(all_normed[stream], keyval_weight[stream]).astype(low)
                for stream in range(2)
            ],
            axis=0,
        )
        key_rows = joined[:, :head_dim]
        values = joined[:, head_dim:]
        queries = jnp.concatenate(
            [
                jnp.concatenate(
                    [
                        (product(all_normed[stream], part) * scaling).astype(low)
                        for part in query_weight[stream]
                    ],
                    axis=1,
                )
                for stream in range(2)
            ],
            axis=0,
        ).reshape(total_rows, -1, head_dim)
        offsets = [0]
        for unused, mask in narrow_links:
            offsets = offsets + [offset ^ mask for offset in offsets]
        owners = at["narrow"] ^ jnp.array(offsets, jnp.int32)

        def reorder(ids):
            return jnp.take(ids.reshape(n_narrow, -1), owners, axis=0).reshape(-1)

        blocks = jnp.concatenate(
            [reorder(prefix_block[0]), reorder(action_block[0]) + PREFIX_BLOCKS]
        )
        positions = (owners[:, None] * own + jnp.arange(own, dtype=jnp.int32)[None]).reshape(-1)
        usable = jnp.concatenate(
            [
                positions < valid_len[0],
                jnp.ones((total_rows - prefix_len,), dtype=jnp.bool_),
            ]
        )
        allowed = (blocks[None, :] <= blocks[:, None]) & usable[None, :]
        scores = masked_scores(queries, key_rows, allowed)
        highest = jnp.max(scores, axis=-1, keepdims=True)
        exponent = jnp.exp(scores - highest)
        denominator = jnp.sum(exponent, axis=-1, keepdims=True)
        log_total = highest + jnp.log(denominator)
        attention = (exponent / denominator).astype(low)
        mixed_all = jnp.einsum("hqk,kd->qhd", attention, values, preferred_element_type=wider)
        mixed_all = mixed_all.astype(low).reshape(total_rows, -1)
        mixed_rows = [mixed_all[:prefix_len], mixed_all[prefix_len:]]
        attended_all = (
            jnp.concatenate(
                [
                    cols_contract(mixed_rows[stream], out_weight[stream]).astype(low)
                    for stream in range(2)
                ],
                axis=1,
            )
        )
        attended_events = []
        attended_all = tie(attended_all, packets[n_wide // 2], *grad_events)
        attended = scatter_rows(attended_all, [core, across], attended_events)
        send_packets(share(7, 8), weight_packet, attended_events[1])
        send_packets(share(3, 4), weight_packet, attended_events[1])
        inputs = [x_prefix.astype(wider), x_action.astype(wider)]
        middle = [
            rows + part for rows, part in zip(inputs, streams(attended), strict=True)
        ]
        normed2 = jnp.concatenate(
            [rms_norm(middle[stream], second_gain[stream]).astype(low) for stream in range(2)],
            axis=1,
        )
        token_events = []
        normed2 = tie(normed2, *(packets[k] for k in share(6, 7) + share(2, 3)))
        near = gather_all(normed2, token_events, True)
        if copying:
            other_most = hop(jnp.concatenate(near[:3], axis=0), core)
            token_far = [(other_most, i) for i in range(3)] + [(hop(near[3], core), 0)]
        else:
            token_far = [(hop(rows, core), 0) for rows in near]
        send_packets(share(5, 6), weight_packet, token_events[-1])
        send_packets(share(0, 2), weight_packet, token_events[-1])
        if aligned:
            feed_weights = copy_blocks(
                packet_plan(
                    False,
                    lambda k: packet_places(
                        k,
                        lambda k, d, f, ref: (block(ref[k], d), span(0, f)),
                        lambda k, d, f, ref: (block(ref[k], d), span(f, f)),
                        lambda k, d, f, part, ref: (span(part * d, d), block(ref[k], d)),
                        (0, 0, 1, 2, 2, 3),
                    ),
                ),
                peers,
                [packets[k] for k in range(n_wide)],
                [
                    (depth[0] * n_wide, 2 * units[0]),
                    (units[0], depth[0] * n_wide),
                    (depth[1] * n_wide, 2 * units[1]),
                    (units[1], depth[1] * n_wide),
                ],
                "unpack_weights",
            )
        else:
            gate_up_weight = [jnp.zeros((depth[i] * n_wide, 2 * units[i]), low) for i in range(2)]
            down_weight = [jnp.zeros((units[i], depth[i] * n_wide), low) for i in range(2)]
            for k, packet in packets.items():
                peer = at["wide"] ^ k
                parts = unpack(packet)
                for i in range(2):
                    gate_up_weight[i] = lax.dynamic_update_slice_in_dim(
                        gate_up_weight[i],
                        jnp.concatenate(parts[3 * i : 3 * i + 2], axis=1),
                        peer * depth[i],
                        0,
                    )
                    down_weight[i] = lax.dynamic_update_slice_in_dim(
                        down_weight[i], parts[3 * i + 2], peer * depth[i], 1
                    )
            feed_weights = [gate_up_weight[0], down_weight[0], gate_up_weight[1], down_weight[1]]

        size = near[0].shape[0]
        feed = functools.partial(
            feed_forward,
            weights=feed_weights,
            size=size,
            total=n_all * own,
            n_copied=4 if copying else 0,
        )
        token_pieces = [(rows, 0) for rows in near] + [token_far[3], *token_far[:3]]
        grad_pieces = [*grad_near, grad_far[3], *grad_far[:3]]
        kept, back_most, out_most = feed(token_pieces[:3], grad_pieces[:3], kept=[], first=0)
        kept, back_corner, out_corner = feed(
            token_pieces[3:5], grad_pieces[3:5], kept=kept, first=3
        )
        kept, back_far, out_far = feed(token_pieces[5:], grad_pieces[5:], kept=kept, first=5)
        hidden_rows, both_rows = kept[-4::2], kept[-3::2]
        if not copying:
            gate_up_grad = [0.0, 0.0]
            down_grad = [0.0, 0.0]
            for i, ((token, token_at), (grad, grad_at)) in enumerate(
                zip(token_pieces, grad_pieces, strict=True)
            ):
                rows = slice(i * size, (i + 1) * size)
                token = streams(token[token_at * size : (token_at + 1) * size])
                grad = streams(grad[grad_at * size : (grad_at + 1) * size])
                for j in range(2):
                    gate_up_grad[j] = gate_up_grad[j] + rows_contract(token[j], both_rows[j][rows])
                    down_grad[j] = down_grad[j] + rows_contract(hidden_rows[j][rows], grad[j])
            gate_up_grad = [grad.astype(low) for grad in gate_up_grad]
            down_grad = [grad.astype(low) for grad in down_grad]
            back_corner, back_far, out_corner, out_far, *held = join(
                back_corner, back_far, out_corner, out_far, *gate_up_grad, *down_grad
            )
            gate_up_grad, down_grad = held[:2], held[2:]
        back_events = []
        dnormed2_packed = scatter_all(
            back_most, back_far, back_corner[:size], back_corner[size:], back_events, True
        )
        dnormed2 = streams(dnormed2_packed)
        mlp_out = streams(
            scatter_all(
                out_most, out_far, out_corner[:size], out_corner[size:], [], False, back_events[1]
            )
        )
        if copying:
            gate_up_grad = [rows_contract(kept[i], both_rows[i]) for i in range(2)]
            down_grad = [rows_contract(hidden_rows[i], kept[2 + i]) for i in range(2)]
            gate_up_grad = [grad.astype(low) for grad in gate_up_grad]
            down_grad = [grad.astype(low) for grad in down_grad]

        def gradient_packet(k):
            peer = at["wide"] ^ k
            parts = []
            for i in range(2):
                both = lax.dynamic_slice_in_dim(gate_up_grad[i], peer * depth[i], depth[i], 0)
                down = lax.dynamic_slice_in_dim(down_grad[i], peer * depth[i], depth[i], 1)
                parts += [both[:, : units[i]], both[:, units[i] :], down]
            return pack(parts)

        if aligned:
            packets = copy_blocks(
                packet_plan(
                    True,
                    lambda k: packet_places(
                        k,
                        lambda k, d, f, ref: (block(ref[k], d), span(0, f)),
                        lambda k, d, f, ref: (block(ref[k], d), span(f, f)),
                        lambda k, d, f, part, ref: (span(part * d, d), block(ref[k], d)),
                        (0, 0, 1, 2, 2, 3),
                    ),
                ),
                peers,
                [gate_up_grad[0], down_grad[0], gate_up_grad[1], down_grad[1]],
                [packet_shape] * n_wide,
                "pack_gradients",
            )
            packets = dict(enumerate(packets))
            gradient_packet = packets.get
        else:
            packets = {0: gradient_packet(0)}
        send_packets(share(4, 5), gradient_packet)
        send_packets(share(2, 3), gradient_packet)
        send_packets(share(6, 7), gradient_packet, back_events[1])
        send_packets(share(0, 2), gradient_packet, back_events[-1])
        send_packets(share(5, 6), gradient_packet, back_events[-1])
        outputs = [(middle[stream] + mlp_out[stream]).astype(low) for stream in range(2)]
        dmiddle = []
        grad_second = []
        for stream, dout_part in enumerate(streams(dout)):
            from_norm, gain_part = norm_back(middle[stream], second_gain[stream], dnormed2[stream])
            dmiddle.append(dout_part + from_norm)
            grad_second.append(gain_part)
        att_events = []
        grad_att = streams(
            gather_rows(
                tie(
                    jnp.concatenate([part.astype(low) for part in dmiddle], axis=1),
                    *(packets[k] for k in share(4, 5) + share(2, 3)),
                ),
                narrow_links,
                att_events,
            )
        )
        send_packets(share(7, 8), gradient_packet, att_events[0])
        send_packets(share(3, 4), gradient_packet, att_events[0])

        def return_wide(parts, links):
            blocks = jnp.concatenate(
                [part.astype(low).reshape(n_wide, -1, part.shape[1]) for part in parts], axis=1
            )
            return scatter_blocks(blocks, links, at)

        out_grads = return_wide(
            [rows_contract(grad_att[stream], mixed_rows[stream]) for stream in range(2)],
            wide_links[::-1],
        )
        grad_out_w = [out_grads[: query_depth[0]].T, out_grads[query_depth[0] :].T]
        dmixed = jnp.concatenate(
            [product(grad_att[stream], out_weight[stream]) for stream in range(2)],
            axis=0,
        )
        dmixed = dmixed.astype(low).reshape(total_rows, -1, head_dim)
        recomputed = jnp.exp(masked_scores(queries, key_rows, allowed) - log_total)
        dprobs = jnp.einsum("qhd,kd->hqk", dmixed, values, preferred_element_type=wider)
        row_inner = jnp.sum(recomputed * dprobs, axis=-1, keepdims=True)
        dscores = (recomputed * (dprobs - row_inner)).astype(low)
        dquery = jnp.einsum("hqk,kd->qhd", dscores, key_rows, preferred_element_type=wider)
        dquery = (dquery.astype(low) * scaling).reshape(total_rows, -1)
        grad_key = jnp.einsum("hqk,qhd->kd", dscores, queries, preferred_element_type=wider)
        dvalue = jnp.einsum(
            "hqk,qhd->kd", recomputed.astype(low), dmixed, preferred_element_type=wider
        )
        grad_keyval = jnp.concatenate([grad_key, dvalue], axis=1).astype(low)
        dquery_rows = [dquery[:prefix_len], dquery[prefix_len:]]
        keyval_rows = [grad_keyval[:prefix_len], grad_keyval[prefix_len:]]
        query_links = [[side] + far[::-1], far[::-1] + [side]]
        query_grads = jnp.concatenate(
            [
                return_wide(
                    [
                        rows_contract(
                            all_normed[stream],
                            dquery_rows[stream][:, part * query_half : (part + 1) * query_half],
                        )
                        for stream in range(2)
                    ],
                    query_links[part],
                )
                for part in range(2)
            ],
            axis=1,
        )
        grad_query_w = [query_grads[: query_depth[0]], query_grads[query_depth[0] :]]
        wide_mlp = []
        for i, (gate_w, down_w) in enumerate(((wg_prefix, wd_prefix), (wg_action, wd_action))):
            wide_mlp += [
                jnp.zeros(gate_w.shape, wider),
                jnp.zeros(gate_w.shape, wider),
                jnp.zeros(down_w.shape, wider),
            ]
        for k, packet in packets.items():
            peer = at["wide"] ^ k
            parts = unpack(packet)
            for i in range(6):
                wide_mlp[i] = lax.dynamic_update_slice_in_dim(
                    wide_mlp[i],
                    parts[i].astype(wider),
                    peer * units[i // 3],
                    0 if i % 3 == 2 else 1,
                )

        dnormed_parts = []
        grad_first = []
        for stream in range(2):
            dnormed = cols_contract(keyval_rows[stream], keyval_weight[stream])
            for part in range(2):
                dnormed = dnormed + cols_contract(
                    dquery_rows[stream][:, part * query_half : (part + 1) * query_half],
                    query_weight[stream][part],
                )
            wide_rows = item_rows[stream].astype(wider)
            unit_rows = wide_rows * lax.rsqrt(
                jnp.mean(wide_rows * wide_rows, axis=-1, keepdims=True) + epsilon
            )
            grad_first.append(jnp.sum(dnormed * unit_rows, axis=0))
            dnormed_parts.append(dnormed.astype(low))
        dnormed = streams(
            scatter_rows(jnp.concatenate(dnormed_parts, axis=1), [core, across])
        )
        grad_inputs = [
            dmiddle[stream] + norm_back(inputs[stream], first_gain[stream], dnormed[stream])[0]
            for stream in range(2)
        ]
        gain_grads = jnp.concatenate(
            [
                part.reshape(n_all, -1)
                for part in (grad_first[0], grad_second[0], grad_first[1], grad_second[1])
            ],
            axis=1,
        )
        shared_grads = scatter_blocks(
            jnp.concatenate(
                [
                    rows_contract(all_normed[stream], keyval_rows[stream])
                    .astype(low)
                    .reshape(n_all, -1, 2 * head_dim)
                    for stream in range(2)
                ]
                + [pad_gains(gain_grads.astype(low))],
                axis=1,
            ),
            [core, across, side] + far[::-1],
            at,
        )
        grad_keyval_w = [
            shared_grads[: keyval_rows_of[0]],
            shared_grads[keyval_rows_of[0] : gain_start],
        ]
        gain_grads = shared_grads[gain_start]
        small = [
            gain_grads[stop - size : stop]
            for stop, size in zip(gain_stops, gain_sizes, strict=True)
        ]
        weights = [
            (
                grad_query_w[i],
                grad_keyval_w[i][:, :head_dim],
                grad_keyval_w[i][:, head_dim:],
                grad_out_w[i],
                *wide_mlp[3 * i : 3 * i + 3],
                small[2 * i],
                small[2 * i + 1],
            )
            for i in range(2)
        ]
        return (*outputs, *grad_inputs, *weights[0], *weights[1])

    return local


def solution(mesh):
    rows = P(BOTH, None)
    block = P("wide", "narrow")
    turned = P("narrow", "wide")
    vector = P(BOTH)
    weights = (block, rows, rows, turned, block, block, turned, vector, vector)
    return jax.shard_map(
        make_local(mesh.shape["wide"], mesh.shape["narrow"]),
        mesh=mesh,
        in_specs=(
            rows,
            rows,
            rows,
            rows,
            P("wide", None),
            P("wide", None),
            P("wide"),
            P("wide"),
            *weights,
            *weights,
        ),
        out_specs=(rows, rows, rows, rows, *weights, *weights),
        check_vma=False,
    )
```
